32 devices in a mesh: au: 4 (over z), vert: 4 (over x, core), ch: 2 (over y).
Axes of the slice: x: 2, y: 2, z: 4, core: 2. Of those that a mesh axis runs over, the one named last changes fastest.
Arguments:
- visibilities: bfloat16 [512, 8, 512], P(('au', 'vert'), None, 'ch'), may hold values from -6 to 6
- tracks: bfloat16 [512, 2, 8], P(('au', 'vert')), may hold values from -10 to 10
- offset_u: int32 [512], P(('au', 'vert')), may hold values from 0 to 255
- offset_v: int32 [512], P(('au', 'vert')), may hold values from 0 to 255
- heading: int32 [512, 1], P(('au', 'vert')), may hold values from 0 to 4; in each aligned block of 32 rows (0 to 31, 32 to 63, ...) at most 8 rows name the same one
- baseline: int32 [512], P(('au', 'vert')), may hold values from 0 to 2015
- station_pair: int32 [2, 2016], replicated, may hold values from 0 to 63, as said below
- screens: bfloat16 [64, 4, 4096], P('ch'), may hold values from -4.1875 to 4.1875
Outputs:
- band_grid: float32 [2, 8, 1024, 1024], P('ch', None, 'au', 'vert')
The draws below stay inside these ranges and needn't reach their ends.
Inputs may be any that keep to these rules, and one draw needn't show every extreme that they name: Within the blocks of one tile (aligned runs of 32 rows) no heading occurs more than 8 times. `station_pair`: the two stations of a baseline differ.
All inputs are finite; a program needn't handle non-finite values.
Results may differ from the reference program's by a relative error of at most 0.0065.
Values may be sent and summed in bfloat16 or wider, within the bound.
A program may use at most 128 MiB of HBM per device.

```python
import math
import jax
import jax.numpy as jnp
import numpy as np
from jax import lax

S = 64
CH_DEV = 32
TB = 8
STATION_COUNT = 64
B_DEV = 32
TU = 256
TV = 256
K = 256
CHANNELS = 64
BASELINE_COUNT = 2016
BLOCK_COUNT = 512
NU = 1024
NV = 1024
N_AU = 4
N_VERT = 4
N_CH = 2


def draw_station_pair(key, part):
    key_leading, key_spacing = jax.random.split(jax.random.fold_in(key, 17))
    leading_station = jax.random.randint(key_leading, (BASELINE_COUNT,), 0, STATION_COUNT)
    station_spacing = jax.random.randint(key_spacing, (BASELINE_COUNT,), 1, STATION_COUNT)
    second_station = (leading_station + station_spacing) % STATION_COUNT
    return jnp.stack([leading_station, second_station]).astype(jnp.int32)


def place_ends(result, stream_key, least, largest):
    place = [jax.random.randint(jax.random.fold_in(stream_key, axis), (), 0, length) for axis, length in enumerate(result.shape)]
    main_axis = result.shape.index(max(result.shape))
    neighbour = place[:main_axis] + [(place[main_axis] + 1) % result.shape[main_axis]] + place[main_axis + 1:]
    return result.at[tuple(place)].set(least).at[tuple(neighbour)].set(largest)


def levels(stream_key, shape, shards, least, top_value):
    factor_of, own = 1.0, jax.random.fold_in(stream_key, 6)
    for dim, blocks in shards:
        steps = jnp.exp(jax.random.uniform(jax.random.fold_in(own, dim), (blocks,), jnp.float32, least / len(shards), top_value / len(shards)))
        factor_of = factor_of * jnp.repeat(steps, shape[dim] // blocks).reshape([-1 if axis == dim else 1 for axis in range(len(shape))])
    return factor_of


def deal_out(rng, own, number, rows, count, top, bound, skew):
    ranking = jax.random.permutation(rng, count)
    heavy_load, usual = portions_of(count, rows * top, bound, skew, True), portions_of(count, rows * top, bound, skew, False)
    places = jnp.arange(count)

    def named(sizes, turn):
        used = int((sizes > 0).sum())
        fixed = max(1, used // 4)
        passed = fixed + (places - fixed + turn * (used - fixed)) % max(1, count - fixed)
        return jnp.zeros((count,), jnp.int32).at[ranking[jnp.where(places < fixed, places, passed)]].set(jnp.asarray(sizes, jnp.int32))

    sizes = jnp.where(number % 4 == 0, named(heavy_load, number // 4), named(usual, number - number // 4 - 1))
    mixed = jax.random.permutation(jax.random.fold_in(own, 3), count)
    donor, receiver = mixed[0:count // 2 * 2:2], mixed[1:count // 2 * 2:2]
    room = jnp.minimum(sizes[donor] - 1, bound - sizes[receiver]) // 2
    room = jnp.where((donor == ranking[0]) | (receiver == ranking[0]) | (sizes[receiver] == 0), 0, jnp.maximum(room, 0))
    passed = jax.random.randint(jax.random.fold_in(own, 4), (count // 2,), 0, 1 << 20) % (room + 1)
    sizes = sizes.at[donor].add(-passed).at[receiver].add(passed)
    items = jnp.searchsorted(jnp.cumsum(sizes), jnp.arange(rows * top), side="right").astype(jnp.int32)
    listing = items.reshape(top, rows).T
    listing = listing[jax.random.permutation(jax.random.fold_in(own, 1), rows)]
    turn = jax.random.randint(jax.random.fold_in(own, 2), (rows, 1), 0, top)
    return jnp.take_along_axis(listing, (jnp.arange(top)[None, :] + turn) % top, axis=1)


def portions_of(count, total, reach, slope, full):
    loads = [(1 << 20) // math.isqrt(standing ** slope) + 1 for standing in range(1, count + 1)]
    largest = reach if full else min(reach, max(-(-total // count), total * loads[0] // sum(loads)))
    least = 1 if total - largest >= count - 1 else 0
    given, spare = [largest] + [least] * (count - 1), total - largest - least * (count - 1)
    while spare > 0:
        candidates = [i for i in range(1, count) if given[i] < largest] or [i for i in range(1, count) if given[i] < reach]
        pool, remaining = sum([loads[i] for i in candidates]), spare
        for i in candidates:
            addition = min(reach - given[i], max(1, remaining * loads[i] // pool), spare)
            given[i] = given[i] + addition
            spare = spare - addition
    return np.array(given)


def bell_draw(stream_key, dims, spread, most, cuts=(), kind=jnp.bfloat16):
    gain = levels(stream_key, dims, cuts, -0.22, 0.18) if cuts else 1.0
    entries = jax.random.normal(stream_key, dims, jnp.float32) * spread * gain
    return jnp.minimum(jnp.maximum(entries, -most), most).astype(kind)


def setup_inputs(seed: int = 0) -> dict:
    splits = jax.random.split(jax.random.key(seed), 9)
    visibilities = bell_draw(splits[0], (BLOCK_COUNT, 8, N_CH * K), 1.0, 6.0, ((0, 16), (2, 2)))
    tracks = jnp.clip(jax.random.uniform(splits[1], (BLOCK_COUNT, 2, TB), jnp.float32, -10.0, 10.0) * levels(splits[1], (BLOCK_COUNT, 2, TB), ((0, 16),), -0.4, 0.0), -10.0, 10.0).astype(jnp.bfloat16)
    offset_u = place_ends(jax.random.randint(splits[2], (BLOCK_COUNT,), 0, TU), jax.random.fold_in(splits[2], 1), 0, TU - 1).astype(jnp.int32)
    offset_v = place_ends(jax.random.randint(splits[3], (BLOCK_COUNT,), 0, TV), jax.random.fold_in(splits[3], 1), 0, TV - 1).astype(jnp.int32)
    heading_keys = jax.random.split(jax.random.fold_in(splits[4], 1), BLOCK_COUNT // B_DEV)
    heading_turns = jax.random.permutation(jax.random.fold_in(splits[4], 3), BLOCK_COUNT // B_DEV)
    heading = jax.vmap(lambda own, number: deal_out(jax.random.fold_in(splits[4], 2), own, number, B_DEV, 5, 1, B_DEV // 4, 2))(heading_keys, heading_turns).reshape((BLOCK_COUNT, 1))
    baseline = place_ends(jax.random.randint(splits[5], (BLOCK_COUNT,), 0, BASELINE_COUNT), jax.random.fold_in(splits[5], 1), 0, BASELINE_COUNT - 1).astype(jnp.int32)
    station_pair = draw_station_pair(jax.random.fold_in(splits[8], 71), 0)
    screens = bell_draw(splits[7], (STATION_COUNT, 4, S * S), 0.7, 4.1875, ((0, 2),))
    return {"visibilities": visibilities, "tracks": tracks, "offset_u": offset_u, "offset_v": offset_v, "heading": heading, "baseline": baseline, "station_pair": station_pair, "screens": screens}


def product_full(pattern, first_op, second_op):
    return jnp.einsum(pattern, first_op.astype(jnp.float32), second_op.astype(jnp.float32))

def phase_tables(track_rows, band_index, channels):
    channel = band_index * CH_DEV + jnp.arange(CH_DEV, dtype=jnp.int32)
    freq_ratio = 1.0 + channel.astype(jnp.float32) / jnp.float32(2 * channels)
    position = track_rows.astype(jnp.float32)[:, :, :, None] * freq_ratio[None, None, None, :]
    position = position.reshape(track_rows.shape[0], 2, TB * CH_DEV)
    pixels = (jnp.arange(S, dtype=jnp.float32) - jnp.float32(S // 2)) / jnp.float32(S)
    angles = jnp.float32(2.0 * math.pi) * position[:, :, :, None] * pixels[None, None, None, :]
    return (jnp.cos(angles).astype(jnp.bfloat16), jnp.sin(angles).astype(jnp.bfloat16))

def dft_table():
    centred = jnp.arange(S, dtype=jnp.int32) - S // 2
    product = centred[:, None] * centred[None, :] % S
    angles = jnp.float32(2.0 * math.pi / S) * product.astype(jnp.float32)
    root_scale = jnp.float32(1.0 / math.sqrt(S))
    return ((jnp.cos(angles) * root_scale).astype(jnp.bfloat16), (-jnp.sin(angles) * root_scale).astype(jnp.bfloat16))

def make_subgrids(samples, track_rows, leading_station, second_station, screens, band_index, channels):
    number = samples.shape[0]
    cos_table, sin_table = phase_tables(track_rows, band_index, channels)
    cos_u = cos_table[:, 0].astype(jnp.float32)[:, None]
    sin_u = sin_table[:, 0].astype(jnp.float32)[:, None]
    cos_v = cos_table[:, 1]
    sin_v = sin_table[:, 1]
    vis_re = samples[:, 0::2].astype(jnp.float32)[..., None]
    vis_im = samples[:, 1::2].astype(jnp.float32)[..., None]
    weigh_re = (vis_re * cos_u - vis_im * sin_u).astype(jnp.bfloat16)
    weigh_im = (vis_re * sin_u + vis_im * cos_u).astype(jnp.bfloat16)
    norm_scale = jnp.float32(1.0 / math.sqrt(TB * CH_DEV))
    pattern = 'npkl,nkm->nplm'
    image_re = (product_full(pattern, weigh_re, cos_v) - product_full(pattern, weigh_im, sin_v)) * norm_scale
    image_im = (product_full(pattern, weigh_re, sin_v) + product_full(pattern, weigh_im, cos_v)) * norm_scale
    screen_one = jnp.take(screens, leading_station, axis=0).astype(jnp.float32).reshape(number, 2, 2, S, S)
    screen_two = jnp.take(screens, second_station, axis=0).astype(jnp.float32).reshape(number, 2, 2, S, S)
    one_re = screen_one[:, :, 0][:, :, None]
    one_im = screen_one[:, :, 1][:, :, None]
    two_re = screen_two[:, :, 0][:, None, :]
    two_im = screen_two[:, :, 1][:, None, :]
    gain_re = (one_re * two_re + one_im * two_im).reshape(number, 4, S, S)
    gain_im = (one_im * two_re - one_re * two_im).reshape(number, 4, S, S)
    fixed_re = (image_re * gain_re - image_im * gain_im).astype(jnp.bfloat16)
    fixed_im = (image_re * gain_im + image_im * gain_re).astype(jnp.bfloat16)
    dft_re, dft_im = dft_table()
    left = 'kl,nplm->npkm'
    half_re = (product_full(left, dft_re, fixed_re) - product_full(left, dft_im, fixed_im)).astype(jnp.bfloat16)
    half_im = (product_full(left, dft_re, fixed_im) + product_full(left, dft_im, fixed_re)).astype(jnp.bfloat16)
    right = 'npkm,jm->npkj'
    out_re = product_full(right, half_re, dft_re) - product_full(right, half_im, dft_im)
    out_im = product_full(right, half_re, dft_im) + product_full(right, half_im, dft_re)
    return jnp.stack([out_re, out_im], axis=2).reshape(number, 8, S, S)

def reference(visibilities, tracks, offset_u, offset_v, heading, baseline, station_pair, screens):
    step_u = jnp.array([0, 1, -1, 0, 0], dtype=jnp.int32)
    step_v = jnp.array([0, 0, 0, 1, -1], dtype=jnp.int32)
    first_all = station_pair[0][baseline].astype(jnp.int32)
    second_all = station_pair[1][baseline].astype(jnp.int32)
    head_codes = heading[:, 0].astype(jnp.int32)
    band_grids = []
    for band_index in range(N_CH):
        band_vis = visibilities[:, :, band_index * K:(band_index + 1) * K]

        def one_source(source, padded):
            source = source.astype(jnp.int32)
            first_row = source * B_DEV

            def own_rows(array):
                return lax.dynamic_slice_in_dim(array, first_row, B_DEV, 0)
            subgrids = make_subgrids(own_rows(band_vis), own_rows(tracks), own_rows(first_all), own_rows(second_all), screens, band_index, CHANNELS)
            home_u = source // N_VERT
            home_v = source % N_VERT
            head_rows = own_rows(head_codes)
            dest_u = (home_u + step_u[head_rows]) % N_AU
            dest_v = (home_v + step_v[head_rows]) % N_VERT
            cell_u = (dest_u * TU + own_rows(offset_u)).astype(jnp.int32)
            cell_v = (dest_v * TV + own_rows(offset_v)).astype(jnp.int32)

            def add_one(slot_index, canvas):
                corner = (jnp.int32(0), cell_u[slot_index].astype(jnp.int32), cell_v[slot_index].astype(jnp.int32))
                window = lax.dynamic_slice(canvas, corner, (8, S, S))
                return lax.dynamic_update_slice(canvas, window + subgrids[slot_index], corner)
            return lax.fori_loop(0, B_DEV, add_one, padded)
        padded = lax.fori_loop(0, N_AU * N_VERT, one_source, jnp.zeros((8, NU + S, NV + S), jnp.float32))
        folded = padded[:, :NU, :]
        folded = folded.at[:, :S, :].add(padded[:, NU:, :])
        band_grid = folded[:, :, :NV]
        band_grid = band_grid.at[:, :, :S].add(folded[:, :, NV:])
        band_grids.append(band_grid)
    return jnp.stack(band_grids)
```

```python
import functools
import math

import jax
import jax.numpy as jnp
import ml_dtypes
import numpy as np
from jax import lax
from jax.experimental import pallas as pl
from jax.experimental.pallas import tpu as pltpu
from jax.sharding import PartitionSpec as P

S = 64
CH_DEV = 32
TB = 8
K = TB * CH_DEV
B_DEV = 32
CAP = B_DEV // 4
SLOTS = 5 * CAP
TU = 256
TV = 256
ROWS = 72
MESH = pl.DeviceIdType.MESH
BF = jnp.bfloat16
F32 = jnp.float32


def series(values, degree):
    nodes = (np.cos(np.pi * (np.arange(400) + 0.5) / 400) + 1.0) * 0.125
    fitted = np.polynomial.chebyshev.Chebyshev.fit(nodes, values(nodes), degree, domain=[0, 0.25])
    return [float(c) for c in fitted.convert(kind=np.polynomial.Polynomial).coef]


COS_COEF = series(lambda q: np.cos(2 * np.pi * np.sqrt(q)), 7)
SIN_COEF = series(lambda q: np.sin(2 * np.pi * np.sqrt(q)) / np.sqrt(q), 6)


def horner(coefs, q):
    total = jnp.full_like(q, coefs[-1])
    for c in coefs[-2::-1]:
        total = total * q + jnp.float32(c)
    return total


def dft_tables():
    centred = np.arange(S) - S // 2
    product = (centred[:, None] * centred[None, :]) % S
    angles = np.float32(2.0 * math.pi / S) * product.astype(np.float32)
    scale = np.float32(1.0 / math.sqrt(S))
    re = (np.cos(angles) * scale).astype(ml_dtypes.bfloat16).astype(np.float32)
    im = (-np.sin(angles) * scale).astype(ml_dtypes.bfloat16).astype(np.float32)
    return re, im


def right_table():
    re, im = dft_tables()
    norm = np.float32(1.0 / math.sqrt(K))
    table = np.zeros((2 * S, 512), np.float32)
    table[:S, :S] = re.T * norm
    table[S:, :S] = -im.T * norm
    table[:S, 256 : 256 + S] = im.T * norm
    table[S:, 256 : 256 + S] = re.T * norm
    return table


def left_table():
    re, im = dft_tables()
    table = np.zeros((8, 2, ROWS, 2 * S), np.float32)
    for shift in range(8):
        table[shift, 0, shift : shift + S, :S] = re
        table[shift, 0, shift : shift + S, S:] = -im
        table[shift, 1, shift : shift + S, :S] = im
        table[shift, 1, shift : shift + S, S:] = re
    return table.reshape(8, 2 * ROWS, 2 * S).astype(ml_dtypes.bfloat16)


def pack_kernel(head, off_u, off_v, base, pairs, data, out_data, out_meta, counts):
    for h in range(5):
        counts[h] = 0
    out_meta[...] = jnp.zeros_like(out_meta)
    lane = lax.broadcasted_iota(jnp.int32, (1, 128), 1)

    def one(b, carry):
        h = head[b]
        slot = h * CAP + counts[h]
        counts[h] = counts[h] + 1
        out_data[slot] = data[b]
        label = base[b]
        row = jnp.where(lane == 0, 1, 0)
        row = jnp.where(lane == 1, off_u[b], row)
        row = jnp.where(lane == 2, off_v[b], row)
        row = jnp.where(lane == 3, pairs[0, label], row)
        row = jnp.where(lane == 4, pairs[1, label], row)
        out_meta[pl.ds(slot, 1), :] = row
        return carry

    lax.fori_loop(0, B_DEV, one, 0)


def exchange_kernel(data, meta, got_data, got_meta, send_sems, recv_sems):
    au, vert = lax.axis_index("au"), lax.axis_index("vert")
    n_au, n_vert = lax.axis_size("au"), lax.axis_size("vert")
    near = (
        {"au": lax.rem(au + 1, n_au)},
        {"au": lax.rem(au + n_au - 1, n_au)},
        {"vert": lax.rem(vert + 1, n_vert)},
        {"vert": lax.rem(vert + n_vert - 1, n_vert)},
    )
    barrier = pltpu.get_barrier_semaphore()
    for device in near:
        pl.semaphore_signal(barrier, inc=1, device_id=device, device_id_type=MESH)
    pl.semaphore_wait(barrier, 4)
    copies = []
    for i, device in enumerate(near):
        for j, (source, target) in enumerate(((data, got_data), (meta, got_meta))):
            copy = pltpu.make_async_remote_copy(
                src_ref=source.at[pl.ds((i + 1) * CAP, CAP)],
                dst_ref=target.at[pl.ds(i * CAP, CAP)],
                send_sem=send_sems.at[i, j],
                recv_sem=recv_sems.at[i, j],
                device_id=device,
                device_id_type=MESH,
            )
            copy.start()
            copies.append(copy)
    for copy in copies:
        copy.wait()


def border_kernel(edge_u, edge_v, corner, got_u, got_v, got_c, send_sems, recv_sems):
    au, vert = lax.axis_index("au"), lax.axis_index("vert")
    n_au, n_vert = lax.axis_size("au"), lax.axis_size("vert")
    au_next, au_last = lax.rem(au + 1, n_au), lax.rem(au + n_au - 1, n_au)
    vert_next, vert_last = lax.rem(vert + 1, n_vert), lax.rem(vert + n_vert - 1, n_vert)
    targets = ({"au": au_next}, {"vert": vert_next}, {"au": au_next, "vert": vert_next})
    sources = ({"au": au_last}, {"vert": vert_last}, {"au": au_last, "vert": vert_last})
    barrier = pltpu.get_barrier_semaphore()
    for device in sources:
        pl.semaphore_signal(barrier, inc=1, device_id=device, device_id_type=MESH)
    pl.semaphore_wait(barrier, 3)
    copies = []
    for i, (source, target) in enumerate(((edge_u, got_u), (edge_v, got_v), (corner, got_c))):
        copy = pltpu.make_async_remote_copy(
            src_ref=source,
            dst_ref=target,
            send_sem=send_sems.at[i],
            recv_sem=recv_sems.at[i],
            device_id=targets[i],
            device_id_type=MESH,
        )
        copy.start()
        copies.append(copy)
    for copy in copies:
        copy.wait()


def swap_halves(x):
    return pltpu.roll(x, S, x.ndim - 1)


def main_kernel(
    own_meta, got_meta, own_data, got_data, own_screens, got_screens, right, left,
    tile, edge_u, edge_v, corner, data, screens, canvas, mult, listing,
):
    band = lax.axis_index("ch")
    channels = CH_DEV * lax.axis_size("ch")
    data[:CAP] = own_data[:CAP]
    data[CAP:] = got_data[...]
    canvas[...] = jnp.zeros_like(canvas)
    row = lax.broadcasted_iota(jnp.int32, (16, K), 0)
    channel = band * CH_DEV + lax.broadcasted_iota(jnp.int32, (16, K), 1) % CH_DEV
    ratio = 1.0 + channel.astype(F32) / jnp.float32(2 * channels)
    step = jnp.where(row < 8, row.astype(F32) / S, (row - 12).astype(F32) / 8)
    mult[...] = step * ratio
    here = own_screens.shape[0]

    def screen_place(station):
        owner = station // here
        local = station - owner * here
        return jnp.where(owner == band, local, here + local)

    def enlist(slot, count):
        own = slot < CAP

        def read(column):
            mine = own_meta[jnp.minimum(slot, CAP - 1), column]
            other = got_meta[jnp.maximum(slot - CAP, 0), column]
            return jnp.where(own, mine, other)

        @pl.when(read(0) == 1)
        def _():
            listing[0, count] = slot
            listing[1, count] = read(1)
            listing[2, count] = read(2)
            listing[3, count] = screen_place(read(3))
            listing[4, count] = screen_place(read(4))

        return count + read(0)

    number = lax.fori_loop(0, SLOTS, enlist, 0)

    copy_own = own_screens
    copy_got = got_screens
    screens[:here] = copy_own[...]
    screens[here:] = copy_got[...]

    def block(index):
        slot = listing[0, index]
        off_u = listing[1, index]
        off_v = listing[2, index]
        one = listing[3, index]
        two = listing[4, index]
        sample = data[slot].astype(F32)
        turns = jnp.concatenate(
            [sample[8:9] * mult[...], sample[9:10] * mult[...]], axis=0
        )
        frac = turns - jnp.floor(turns + 0.5)
        square = frac * frac
        cos = horner(COS_COEF, square)
        sin = horner(SIN_COEF, square) * frac

        def phasors(first):
            cos_fine, sin_fine = cos[first : first + 8], sin[first : first + 8]
            all_cos, all_sin = [], []
            for a in range(8):
                at = first + 8 + a
                cos_a, sin_a = cos[at : at + 1], sin[at : at + 1]
                all_cos.append(cos_fine * cos_a - sin_fine * sin_a)
                all_sin.append(sin_fine * cos_a + cos_fine * sin_a)
            return (
                jnp.concatenate(all_cos, axis=0).astype(BF),
                jnp.concatenate(all_sin, axis=0).astype(BF),
            )

        cos_u, sin_u = phasors(0)
        cos_u, sin_u = cos_u.astype(F32), sin_u.astype(F32)
        cos_v, sin_v = phasors(16)
        table_re = jnp.concatenate([cos_v, sin_v], axis=0)
        table_im = jnp.concatenate([-sin_v, cos_v], axis=0)
        weigh_re, weigh_im = [], []
        for p in range(4):
            re, im = sample[2 * p : 2 * p + 1], sample[2 * p + 1 : 2 * p + 2]
            weigh_re.append((re * cos_u - im * sin_u).astype(BF))
            weigh_im.append((re * sin_u + im * cos_u).astype(BF))
        dims = (((1,), (1,)), ((), ()))
        image = lax.dot_general(
            jnp.concatenate(weigh_re, axis=0), table_re, dims, preferred_element_type=F32
        ) + lax.dot_general(
            jnp.concatenate(weigh_im, axis=0), table_im, dims, preferred_element_type=F32
        )
        two_s = [screens[two, f].astype(F32) for f in range(2)]
        fixed = []
        for f in range(2):
            one_s = screens[one, f].astype(F32)
            one_swapped = swap_halves(one_s)
            for e in range(2):
                p = 2 * f + e
                same = one_s * two_s[e]
                cross = one_swapped * two_s[e]
                gain_re = same + swap_halves(same)
                gain_im = swap_halves(cross) - cross
                part = image[p * S : (p + 1) * S]
                fixed.append((part * gain_re + swap_halves(part) * gain_im).astype(BF))
        lanes = off_v // 128
        shift = off_v - lanes * 128
        shifted = jnp.concatenate(
            [
                pltpu.roll(right[:, :256], shift, 1).astype(BF),
                pltpu.roll(right[:, 256:], shift, 1).astype(BF),
            ],
            axis=1,
        )
        half = jnp.dot(
            jnp.concatenate(fixed, axis=0), shifted, preferred_element_type=F32
        ).astype(BF)
        eighth = off_u // 8
        placed = left[off_u - eighth * 8]
        start_u = pl.multiple_of(eighth * 8, 8)
        start_v = pl.multiple_of(lanes * 128, 128)
        for p in range(4):
            part = half[p * S : (p + 1) * S]
            both = jnp.concatenate([part[:, :256], part[:, 256:]], axis=0)
            grid = jnp.dot(placed, both, preferred_element_type=F32)
            for r in range(2):
                where = (2 * p + r, pl.ds(start_u, ROWS), pl.ds(start_v, 256))
                canvas[where] += grid[r * ROWS : (r + 1) * ROWS]

    def loop(index, carry):
        block(index)
        return carry

    lax.fori_loop(0, number, loop, 0)

    tile[...] = canvas[:, :TU, :TV]
    edge_u[...] = canvas[:, TU:, :TV].astype(BF)
    lane = lax.broadcasted_iota(jnp.int32, (1, 1, 128), 2)

    def folded(x):
        middle = x.shape[1] // 2
        return jnp.where(lane < S, x[:, :middle], swap_halves(x[:, middle:])).astype(BF)

    edge_v[...] = folded(canvas[:, :TU, TV:])
    corner[...] = folded(canvas[:, TU:, TV:])


def finish_kernel(tile, got_u, got_v, got_c, out):
    lane = lax.broadcasted_iota(jnp.int32, (1, 1, 128), 2)

    def unfolded(x):
        x = x.astype(F32)
        low = jnp.where(lane < S, x, 0.0)
        high = jnp.where(lane < S, swap_halves(x), 0.0)
        return jnp.concatenate([low, high], axis=1)

    out[...] = tile[...]
    out[:, :S, :] += got_u[...].astype(F32)
    out[:, :, :128] += unfolded(got_v[...])
    out[:, :S, :128] += unfolded(got_c[...])


def body(visibilities, tracks, offset_u, offset_v, heading, baseline, station_pair, screens):
    smem = pl.BlockSpec(memory_space=pltpu.SMEM)
    vmem = pl.BlockSpec(memory_space=pltpu.VMEM)
    anywhere = pl.BlockSpec(memory_space=pl.ANY)
    n_ch = lax.axis_size("ch")
    here = screens.shape[0]

    arranged = (
        screens.reshape(here, 2, 2, S, S).transpose(0, 1, 3, 2, 4).reshape(here, 2, S, 2 * S)
    )
    other = lax.ppermute(arranged, "ch", [(i, (i + 1) % n_ch) for i in range(n_ch)])

    spread = jnp.broadcast_to(tracks[:, :, :, None], (B_DEV, 2, TB, CH_DEV)).reshape(B_DEV, 2, K)
    data = jnp.concatenate([visibilities, spread, jnp.zeros((B_DEV, 6, K), BF)], axis=1)
    packed, meta = pl.pallas_call(
        pack_kernel,
        out_shape=(
            jax.ShapeDtypeStruct((SLOTS, 16, K), BF),
            jax.ShapeDtypeStruct((SLOTS, 128), jnp.int32),
        ),
        in_specs=[smem] * 5 + [vmem],
        out_specs=(vmem, vmem),
        scratch_shapes=[pltpu.SMEM((8,), jnp.int32)],
    )(heading[:, 0], offset_u, offset_v, baseline, station_pair, data)
    got_data, got_meta = pl.pallas_call(
        exchange_kernel,
        out_shape=(
            jax.ShapeDtypeStruct((SLOTS - CAP, 16, K), BF),
            jax.ShapeDtypeStruct((SLOTS - CAP, 128), jnp.int32),
        ),
        in_specs=[anywhere, anywhere],
        out_specs=(anywhere, anywhere),
        scratch_shapes=[pltpu.SemaphoreType.DMA((4, 2)), pltpu.SemaphoreType.DMA((4, 2))],
        compiler_params=pltpu.CompilerParams(collective_id=0, has_side_effects=True),
    )(packed, meta)
    tile, edge_u, edge_v, corner = pl.pallas_call(
        main_kernel,
        out_shape=(
            jax.ShapeDtypeStruct((8, TU, TV), F32),
            jax.ShapeDtypeStruct((8, S, TV), BF),
            jax.ShapeDtypeStruct((8, TU // 2, 128), BF),
            jax.ShapeDtypeStruct((8, S // 2, 128), BF),
        ),
        in_specs=[smem, smem] + [vmem] * 6,
        out_specs=(vmem,) * 4,
        scratch_shapes=[
            pltpu.VMEM((SLOTS, 16, K), BF),
            pltpu.VMEM((2 * here, 2, S, 2 * S), BF),
            pltpu.VMEM((8, TU + S, TV + 128), F32),
            pltpu.VMEM((16, K), F32),
            pltpu.SMEM((8, SLOTS + 8), jnp.int32),
        ],
        compiler_params=pltpu.CompilerParams(vmem_limit_bytes=40 << 20),
    )(
        meta, got_meta, packed, got_data, arranged, other,
        jnp.asarray(right_table()), jnp.asarray(left_table()),
    )
    got_u, got_v, got_c = pl.pallas_call(
        border_kernel,
        out_shape=(
            jax.ShapeDtypeStruct(edge_u.shape, BF),
            jax.ShapeDtypeStruct(edge_v.shape, BF),
            jax.ShapeDtypeStruct(corner.shape, BF),
        ),
        in_specs=[anywhere] * 3,
        out_specs=(anywhere,) * 3,
        scratch_shapes=[pltpu.SemaphoreType.DMA((3,)), pltpu.SemaphoreType.DMA((3,))],
        compiler_params=pltpu.CompilerParams(collective_id=1, has_side_effects=True),
    )(edge_u, edge_v, corner)
    out = pl.pallas_call(
        finish_kernel,
        out_shape=jax.ShapeDtypeStruct((8, TU, TV), F32),
        in_specs=[vmem] * 4,
        out_specs=vmem,
    )(tile, got_u, got_v, got_c)
    return out[None]


def solution(mesh):
    placed = (
        P(("au", "vert"), None, "ch"),
        P(("au", "vert"), None, None),
        P(("au", "vert")),
        P(("au", "vert")),
        P(("au", "vert"), None),
        P(("au", "vert")),
        P(),
        P("ch", None, None),
    )
    return jax.shard_map(
        body, mesh=mesh, in_specs=placed, out_specs=P("ch", None, "au", "vert"), check_vma=False
    )
```

```python
import functools
import math

import jax
import jax.numpy as jnp
import ml_dtypes
import numpy as np
from jax import lax
from jax.experimental import pallas as pl
from jax.experimental.pallas import tpu as pltpu
from jax.sharding import PartitionSpec as P

S = 64
CH_DEV = 32
TB = 8
K = TB * CH_DEV
B_DEV = 32
CAP = B_DEV // 4
SLOTS = 5 * CAP
TU = 256
TV = 256
ROWS = 72
MESH = pl.DeviceIdType.MESH
BF = jnp.bfloat16
F32 = jnp.float32


def series(values, degree):
    nodes = (np.cos(np.pi * (np.arange(400) + 0.5) / 400) + 1.0) * 0.125
    fitted = np.polynomial.chebyshev.Chebyshev.fit(nodes, values(nodes), degree, domain=[0, 0.25])
    return [float(c) for c in fitted.convert(kind=np.polynomial.Polynomial).coef]


COS_COEF = series(lambda q: np.cos(2 * np.pi * np.sqrt(q)), 7)
SIN_COEF = series(lambda q: np.sin(2 * np.pi * np.sqrt(q)) / np.sqrt(q), 6)


def horner(coefs, q):
    total = jnp.full_like(q, coefs[-1])
    for c in coefs[-2::-1]:
        total = total * q + jnp.float32(c)
    return total


def dft_tables():
    centred = np.arange(S) - S // 2
    product = (centred[:, None] * centred[None, :]) % S
    angles = np.float32(2.0 * math.pi / S) * product.astype(np.float32)
    scale = np.float32(1.0 / math.sqrt(S))
    re = (np.cos(angles) * scale).astype(ml_dtypes.bfloat16).astype(np.float32)
    im = (-np.sin(angles) * scale).astype(ml_dtypes.bfloat16).astype(np.float32)
    return re, im


def right_table():
    re, im = dft_tables()
    norm = np.float32(1.0 / math.sqrt(K))
    table = np.zeros((2 * S, 512), np.float32)
    table[:S, :S] = re.T * norm
    table[S:, :S] = -im.T * norm
    table[:S, 256 : 256 + S] = im.T * norm
    table[S:, 256 : 256 + S] = re.T * norm
    return table


def left_table():
    re, im = dft_tables()
    order = np.concatenate([np.arange(0, S, 2), np.arange(1, S, 2)])
    re, im = re[:, order], im[:, order]
    table = np.zeros((8, 2, ROWS, 2 * S), np.float32)
    for shift in range(8):
        table[shift, 0, shift : shift + S, :S] = re
        table[shift, 0, shift : shift + S, S:] = -im
        table[shift, 1, shift : shift + S, :S] = im
        table[shift, 1, shift : shift + S, S:] = re
    return table.reshape(8, 2 * ROWS, 2 * S).astype(ml_dtypes.bfloat16)


def pack_kernel(head, off_u, off_v, base, pairs, data, out_data, out_meta, counts):
    for h in range(5):
        counts[h] = 0
    out_meta[...] = jnp.zeros_like(out_meta)
    lane = lax.broadcasted_iota(jnp.int32, (1, 128), 1)

    def one(b, carry):
        h = head[b]
        slot = h * CAP + counts[h]
        counts[h] = counts[h] + 1
        out_data[slot] = data[b]
        label = base[b]
        row = jnp.where(lane == 0, 1, 0)
        row = jnp.where(lane == 1, off_u[b], row)
        row = jnp.where(lane == 2, off_v[b], row)
        row = jnp.where(lane == 3, pairs[0, label], row)
        row = jnp.where(lane == 4, pairs[1, label], row)
        out_meta[pl.ds(slot, 1), :] = row
        return carry

    lax.fori_loop(0, B_DEV, one, 0)


def exchange_kernel(data, meta, got_data, got_meta, send_sems, recv_sems):
    au, vert = lax.axis_index("au"), lax.axis_index("vert")
    n_au, n_vert = lax.axis_size("au"), lax.axis_size("vert")
    near = (
        {"au": lax.rem(au + 1, n_au)},
        {"au": lax.rem(au + n_au - 1, n_au)},
        {"vert": lax.rem(vert + 1, n_vert)},
        {"vert": lax.rem(vert + n_vert - 1, n_vert)},
    )
    barrier = pltpu.get_barrier_semaphore()
    for device in near:
        pl.semaphore_signal(barrier, inc=1, device_id=device, device_id_type=MESH)
    pl.semaphore_wait(barrier, 4)
    copies = []
    for i, device in enumerate(near):
        for j, (source, target) in enumerate(((data, got_data), (meta, got_meta))):
            copy = pltpu.make_async_remote_copy(
                src_ref=source.at[pl.ds((i + 1) * CAP, CAP)],
                dst_ref=target.at[pl.ds(i * CAP, CAP)],
                send_sem=send_sems.at[i, j],
                recv_sem=recv_sems.at[i, j],
                device_id=device,
                device_id_type=MESH,
            )
            copy.start()
            copies.append(copy)
    for copy in copies:
        copy.wait()


def border_kernel(edge_u, edge_v, corner, got_u, got_v, got_c, send_sems, recv_sems):
    au, vert = lax.axis_index("au"), lax.axis_index("vert")
    n_au, n_vert = lax.axis_size("au"), lax.axis_size("vert")
    au_next, au_last = lax.rem(au + 1, n_au), lax.rem(au + n_au - 1, n_au)
    vert_next, vert_last = lax.rem(vert + 1, n_vert), lax.rem(vert + n_vert - 1, n_vert)
    targets = ({"au": au_next}, {"vert": vert_next}, {"au": au_next, "vert": vert_next})
    sources = ({"au": au_last}, {"vert": vert_last}, {"au": au_last, "vert": vert_last})
    barrier = pltpu.get_barrier_semaphore()
    for device in sources:
        pl.semaphore_signal(barrier, inc=1, device_id=device, device_id_type=MESH)
    pl.semaphore_wait(barrier, 3)
    copies = []
    for i, (source, target) in enumerate(((edge_u, got_u), (edge_v, got_v), (corner, got_c))):
        copy = pltpu.make_async_remote_copy(
            src_ref=source,
            dst_ref=target,
            send_sem=send_sems.at[i],
            recv_sem=recv_sems.at[i],
            device_id=targets[i],
            device_id_type=MESH,
        )
        copy.start()
        copies.append(copy)
    for copy in copies:
        copy.wait()


def swap_halves(x):
    return pltpu.roll(x, S, x.ndim - 1)


def enlist_blocks(own_meta, got_meta, listing):
    def place(slot, own, read, count):
        @pl.when(read(0) == 1)
        def _():
            listing[0, count] = slot
            for column in range(1, 5):
                listing[column, count] = read(column)

        return count + read(0)

    def one_own(slot, count):
        return place(slot, True, lambda column: own_meta[slot, column], count)

    def one_got(slot, count):
        return place(slot + CAP, False, lambda column: got_meta[slot, column], count)

    number = lax.fori_loop(0, CAP, one_own, 0)
    number = lax.fori_loop(0, SLOTS - CAP, one_got, number)

    @pl.when(number % 2 == 1)
    def _():
        for column in range(5):
            listing[column, number] = listing[column, number - 1]
        listing[1, number] = TU + S

    return (number + 1) // 2


def arrange_station(raw, tall):
    value = raw.astype(F32)
    for i in range(S // 2):
        tall[8 * i : 8 * i + 4, :] = value[:, 128 * i : 128 * (i + 1)]
    lane = lax.broadcasted_iota(jnp.int32, (S // 2, 128), 1)
    feeds = []
    for f in range(2):
        re = tall[pl.ds(2 * f, S // 2, stride=8), :]
        im = tall[pl.ds(2 * f + 1, S // 2, stride=8), :]
        even = jnp.where(lane < S, re, swap_halves(im))
        odd = jnp.where(lane < S, swap_halves(re), im)
        feeds.append(jnp.concatenate([even, odd], axis=0).astype(BF))
    return feeds


def image_kernel(
    own_meta_v, got_meta_v, own_data, got_data, own_screens,
    images, arranged,
    own_meta, got_meta, data, raw, tall, mult, listing, sems,
):
    fetch = pltpu.make_async_copy(own_screens, raw, sems.at[0])
    fetch.start()
    meta_copies = [
        pltpu.make_async_copy(own_meta_v.at[:CAP], own_meta, sems.at[1]),
        pltpu.make_async_copy(got_meta_v, got_meta, sems.at[2]),
    ]
    for copy in meta_copies:
        copy.start()
    band = lax.axis_index("ch")
    channels = CH_DEV * lax.axis_size("ch")
    data[:CAP] = own_data[:CAP]
    data[CAP:] = got_data[...]
    row = lax.broadcasted_iota(jnp.int32, (32, K), 0)
    channel = band * CH_DEV + lax.broadcasted_iota(jnp.int32, (32, K), 1) % CH_DEV
    ratio = 1.0 + channel.astype(F32) / jnp.float32(2 * channels)
    coarse = row - 8
    coarse_u = 16 * (coarse % 4) + coarse // 4 - S // 2
    fine_v = row - 16
    coarse_v = (row - 24) * 8 - S // 2
    step = jnp.where(
        row < 16, jnp.where(row < 8, 2 * row, coarse_u), jnp.where(row < 24, fine_v, coarse_v)
    )
    mult[...] = step.astype(F32) / S * ratio
    for copy in meta_copies:
        copy.wait()
    pairs = enlist_blocks(own_meta, got_meta, listing)

    def block(index):
        sample = data[listing[0, index]].astype(F32)
        turns = jnp.concatenate(
            [sample[8:9] * mult[:16], sample[9:10] * mult[16:]], axis=0
        )
        frac = turns - jnp.floor(turns + 0.5)
        square = frac * frac
        cos = horner(COS_COEF, square)
        sin = horner(SIN_COEF, square) * frac

        def phasors(first):
            cos_fine, sin_fine = cos[first : first + 8], sin[first : first + 8]
            all_cos, all_sin = [], []
            for a in range(8):
                at = first + 8 + a
                cos_a, sin_a = cos[at : at + 1], sin[at : at + 1]
                all_cos.append(cos_fine * cos_a - sin_fine * sin_a)
                all_sin.append(sin_fine * cos_a + cos_fine * sin_a)
            return (
                jnp.concatenate(all_cos, axis=0).astype(BF),
                jnp.concatenate(all_sin, axis=0).astype(BF),
            )

        cos_u, sin_u = phasors(0)
        cos_u, sin_u = cos_u.astype(F32), sin_u.astype(F32)
        cos_v, sin_v = phasors(16)
        table_re = jnp.concatenate([cos_v, sin_v], axis=0)
        table_im = jnp.concatenate([-sin_v, cos_v], axis=0)
        weigh_re, weigh_im = [], []
        for p in range(4):
            re, im = sample[2 * p : 2 * p + 1], sample[2 * p + 1 : 2 * p + 2]
            weigh_re.append((re * cos_u - im * sin_u).astype(BF))
            weigh_im.append((re * sin_u + im * cos_u).astype(BF))
        dims = (((1,), (1,)), ((), ()))
        image = lax.dot_general(
            jnp.concatenate(weigh_re, axis=0), table_re, dims, preferred_element_type=F32
        ) + lax.dot_general(
            jnp.concatenate(weigh_im, axis=0), table_im, dims, preferred_element_type=F32
        )
        return image.astype(BF)

    def loop(pair, carry):
        first, second = block(2 * pair), block(2 * pair + 1)
        images[2 * pair] = first
        images[2 * pair + 1] = second
        return carry

    lax.fori_loop(0, pairs, loop, 0)
    fetch.wait()

    def arrange(pair, carry):
        for i in range(2):
            feeds = arrange_station(raw[2 * pair + i], tall.at[i])
            for f in range(2):
                arranged[2 * pair + i, f] = feeds[f]
        return carry

    lax.fori_loop(0, raw.shape[0] // 2, arrange, 0)


def grid_kernel(
    own_meta_v, got_meta_v, images, arranged, near_half, far_half, right_in, left_in,
    tile, edge_u, edge_v, corner,
    own_meta, got_meta, raw, screens, canvas, right, left, tall, listing, sems,
):
    here = arranged.shape[0]
    part_size = here // 2
    meta_copies = [
        pltpu.make_async_copy(own_meta_v.at[:CAP], own_meta, sems.at[0]),
        pltpu.make_async_copy(got_meta_v, got_meta, sems.at[1]),
    ]
    fetches = [
        pltpu.make_async_copy(near_half, raw.at[:part_size], sems.at[2]),
        pltpu.make_async_copy(far_half, raw.at[part_size:], sems.at[3]),
        pltpu.make_async_copy(arranged, screens.at[:here], sems.at[4]),
        pltpu.make_async_copy(right_in, right, sems.at[5]),
        pltpu.make_async_copy(left_in, left, sems.at[6]),
    ]
    for copy in meta_copies + fetches:
        copy.start()
    band = lax.axis_index("ch")
    parity = lax.rem(lax.axis_index("vert"), 2)
    canvas[...] = jnp.zeros_like(canvas)
    for copy in meta_copies:
        copy.wait()
    pairs = enlist_blocks(own_meta, got_meta, listing)
    for copy in fetches:
        copy.wait()

    def arrange(pair, carry):
        for i in range(2):
            feeds = arrange_station(raw[2 * pair + i], tall.at[i])
            for f in range(2):
                screens[here + 2 * pair + i, f] = feeds[f]
        return carry

    lax.fori_loop(0, part_size, arrange, 0)

    def screen_place(station):
        owner = station // here
        local = station - owner * here
        chosen = local // part_size
        moved = here + local % part_size + jnp.where(chosen == parity, 0, part_size)
        return jnp.where(owner == band, local, moved)

    def block(index):
        off_u = listing[1, index]
        off_v = listing[2, index]
        one = screen_place(listing[3, index])
        two = screen_place(listing[4, index])
        two_s = [screens[two, f].astype(F32) for f in range(2)]
        fixed = []
        for f in range(2):
            one_s = screens[one, f].astype(F32)
            one_swapped = swap_halves(one_s)
            for e in range(2):
                p = 2 * f + e
                same = one_s * two_s[e]
                cross = one_swapped * two_s[e]
                gain_re = same + swap_halves(same)
                gain_im = swap_halves(cross) - cross
                part = images[index, p * S : (p + 1) * S].astype(F32)
                fixed.append((part * gain_re + swap_halves(part) * gain_im).astype(BF))
        lanes = off_v // 128
        shift = off_v - lanes * 128
        shifted = jnp.concatenate(
            [
                pltpu.roll(right[:, :256], shift, 1).astype(BF),
                pltpu.roll(right[:, 256:], shift, 1).astype(BF),
            ],
            axis=1,
        )
        half = jnp.dot(
            jnp.concatenate(fixed, axis=0), shifted, preferred_element_type=F32
        ).astype(BF)
        eighth = off_u // 8
        placed = left[off_u - eighth * 8]
        start_u = pl.multiple_of(eighth * 8, 8)
        start_v = pl.multiple_of(lanes * 128, 128)
        grids = []
        for p in range(4):
            part = half[p * S : (p + 1) * S]
            both = jnp.concatenate([part[:, :256], part[:, 256:]], axis=0)
            grids.append(jnp.dot(placed, both, preferred_element_type=F32))
        return start_u, start_v, grids

    def loop(pair, carry):
        for start_u, start_v, grids in [block(2 * pair), block(2 * pair + 1)]:
            for p in range(4):
                for r in range(2):
                    where = (2 * p + r, pl.ds(start_u, ROWS), pl.ds(start_v, 256))
                    canvas[where] += grids[p][r * ROWS : (r + 1) * ROWS]
        return carry

    lax.fori_loop(0, pairs, loop, 0)

    store = pltpu.make_async_copy(canvas.at[:, :TU, :TV], tile, sems.at[7])
    store.start()
    edge_u[...] = canvas[:, TU : TU + S, :TV].astype(BF)
    lane = lax.broadcasted_iota(jnp.int32, (1, 1, 128), 2)

    def folded(x):
        middle = x.shape[1] // 2
        return jnp.where(lane < S, x[:, :middle], swap_halves(x[:, middle:])).astype(BF)

    edge_v[...] = folded(canvas[:, :TU, TV:])
    corner[...] = folded(canvas[:, TU : TU + S, TV:])
    store.wait()


def finish_kernel(tile, got_u, got_v, got_c, out, top, side, sems):
    fetch_top = pltpu.make_async_copy(tile.at[:, :S, :], top, sems.at[0])
    fetch_side = pltpu.make_async_copy(tile.at[:, S:, :128], side, sems.at[1])
    fetch_top.start()
    fetch_side.start()
    lane = lax.broadcasted_iota(jnp.int32, (1, 1, 128), 2)

    def unfolded(x):
        x = x.astype(F32)
        low = jnp.where(lane < S, x, 0.0)
        high = jnp.where(lane < S, swap_halves(x), 0.0)
        return low, high

    low, high = unfolded(got_v[...])
    first, second = unfolded(got_c[...])
    fetch_top.wait()
    top[...] += got_u[...].astype(F32)
    top[:, :, :128] += low[:, :S] + jnp.concatenate([first, second], axis=1)
    store_top = pltpu.make_async_copy(top, out.at[:, :S, :], sems.at[2])
    store_top.start()
    fetch_side.wait()
    side[:, : TU // 2 - S] += low[:, S:]
    side[:, TU // 2 - S :] += high
    store_side = pltpu.make_async_copy(side, out.at[:, S:, :128], sems.at[3])
    store_side.start()
    store_top.wait()
    store_side.wait()


def body(visibilities, tracks, offset_u, offset_v, heading, baseline, station_pair, screens):
    smem = pl.BlockSpec(memory_space=pltpu.SMEM)
    vmem = pl.BlockSpec(memory_space=pltpu.VMEM)
    anywhere = pl.BlockSpec(memory_space=pl.ANY)
    n_ch = lax.axis_size("ch")
    here = screens.shape[0]

    half_size = here // 2
    n_vert = lax.axis_size("vert")
    parity = lax.rem(lax.axis_index("vert"), 2)
    chosen = lax.dynamic_slice_in_dim(screens, parity * half_size, half_size, 0)
    near_half = lax.ppermute(chosen, "ch", [(i, (i + 1) % n_ch) for i in range(n_ch)])
    far_half = lax.ppermute(near_half, "vert", [(i, i ^ 1) for i in range(n_vert)])

    spread = jnp.broadcast_to(tracks[:, :, :, None], (B_DEV, 2, TB, CH_DEV)).reshape(B_DEV, 2, K)
    data = jnp.concatenate([visibilities, spread, jnp.zeros((B_DEV, 6, K), BF)], axis=1)
    packed, meta = pl.pallas_call(
        pack_kernel,
        out_shape=(
            jax.ShapeDtypeStruct((SLOTS, 16, K), BF),
            jax.ShapeDtypeStruct((SLOTS, 128), jnp.int32),
        ),
        in_specs=[smem] * 5 + [vmem],
        out_specs=(vmem, vmem),
        scratch_shapes=[pltpu.SMEM((8,), jnp.int32)],
    )(heading[:, 0], offset_u, offset_v, baseline, station_pair, data)
    got_data, got_meta = pl.pallas_call(
        exchange_kernel,
        out_shape=(
            jax.ShapeDtypeStruct((SLOTS - CAP, 16, K), BF),
            jax.ShapeDtypeStruct((SLOTS - CAP, 128), jnp.int32),
        ),
        in_specs=[vmem, vmem],
        out_specs=(vmem, vmem),
        scratch_shapes=[pltpu.SemaphoreType.DMA((4, 2)), pltpu.SemaphoreType.DMA((4, 2))],
        compiler_params=pltpu.CompilerParams(collective_id=0, has_side_effects=True),
    )(packed, meta)
    images, arranged = pl.pallas_call(
        image_kernel,
        out_shape=(
            jax.ShapeDtypeStruct((SLOTS, 4 * S, 2 * S), BF),
            jax.ShapeDtypeStruct((here, 2, S, 2 * S), BF),
        ),
        in_specs=[vmem] * 4 + [anywhere],
        out_specs=(vmem, vmem),
        scratch_shapes=[
            pltpu.SMEM((CAP, 128), jnp.int32),
            pltpu.SMEM((SLOTS - CAP, 128), jnp.int32),
            pltpu.VMEM((SLOTS, 16, K), BF),
            pltpu.VMEM(screens.shape, BF),
            pltpu.VMEM((2, 4 * S, 128), F32),
            pltpu.VMEM((32, K), F32),
            pltpu.SMEM((8, SLOTS + 8), jnp.int32),
            pltpu.SemaphoreType.DMA((3,)),
        ],
        compiler_params=pltpu.CompilerParams(vmem_limit_bytes=20 << 20),
        cost_estimate=pl.CostEstimate(
            flops=SLOTS * 2 * 256 * 512 * 128 * 8, bytes_accessed=8 << 20, transcendentals=0
        ),
    )(meta, got_meta, packed, got_data, screens)
    tile, edge_u, edge_v, corner = pl.pallas_call(
        grid_kernel,
        out_shape=(
            jax.ShapeDtypeStruct((8, TU, TV), F32),
            jax.ShapeDtypeStruct((8, S, TV), BF),
            jax.ShapeDtypeStruct((8, TU // 2, 128), BF),
            jax.ShapeDtypeStruct((8, S // 2, 128), BF),
        ),
        in_specs=[vmem] * 3 + [anywhere] * 5,
        out_specs=(anywhere, vmem, vmem, vmem),
        scratch_shapes=[
            pltpu.SMEM((CAP, 128), jnp.int32),
            pltpu.SMEM((SLOTS - CAP, 128), jnp.int32),
            pltpu.VMEM(screens.shape, BF),
            pltpu.VMEM((2 * here, 2, S, 2 * S), BF),
            pltpu.VMEM((8, TU + S + ROWS, TV + 128), F32),
            pltpu.VMEM((2 * S, 512), F32),
            pltpu.VMEM((8, 2 * ROWS, 2 * S), BF),
            pltpu.VMEM((2, 4 * S, 128), F32),
            pltpu.SMEM((8, SLOTS + 8), jnp.int32),
            pltpu.SemaphoreType.DMA((8,)),
        ],
        compiler_params=pltpu.CompilerParams(vmem_limit_bytes=28 << 20),
    )(
        meta, got_meta, images, arranged, near_half, far_half,
        jnp.asarray(right_table()), jnp.asarray(left_table()),
    )
    got_u, got_v, got_c = pl.pallas_call(
        border_kernel,
        out_shape=(
            jax.ShapeDtypeStruct(edge_u.shape, BF),
            jax.ShapeDtypeStruct(edge_v.shape, BF),
            jax.ShapeDtypeStruct(corner.shape, BF),
        ),
        in_specs=[vmem] * 3,
        out_specs=(vmem,) * 3,
        scratch_shapes=[pltpu.SemaphoreType.DMA((3,)), pltpu.SemaphoreType.DMA((3,))],
        compiler_params=pltpu.CompilerParams(collective_id=1, has_side_effects=True),
    )(edge_u, edge_v, corner)
    out = pl.pallas_call(
        finish_kernel,
        out_shape=jax.ShapeDtypeStruct((8, TU, TV), F32),
        in_specs=[anywhere] + [vmem] * 3,
        out_specs=anywhere,
        scratch_shapes=[
            pltpu.VMEM((8, S, TV), F32),
            pltpu.VMEM((8, TU - S, 128), F32),
            pltpu.SemaphoreType.DMA((4,)),
        ],
        input_output_aliases={0: 0},
    )(tile, got_u, got_v, got_c)
    return out[None]


def solution(mesh):
    placed = (
        P(("au", "vert"), None, "ch"),
        P(("au", "vert"), None, None),
        P(("au", "vert")),
        P(("au", "vert")),
        P(("au", "vert"), None),
        P(("au", "vert")),
        P(),
        P("ch", None, None),
    )
    return jax.shard_map(
        body, mesh=mesh, in_specs=placed, out_specs=P("ch", None, "au", "vert"), check_vma=False
    )
```

```python
import math

import jax
import jax.numpy as jnp
import ml_dtypes
import numpy as np
from jax import lax
from jax.experimental import pallas as pl
from jax.experimental.pallas import tpu as pltpu
from jax.sharding import PartitionSpec as P

S = 64
CH_DEV = 32
TB = 8
K = TB * CH_DEV
B_DEV = 32
CAP = B_DEV // 4
SLOTS = 5 * CAP
TU = 256
TV = 256
ROWS = 72
LATER = 48
MESH = pl.DeviceIdType.MESH
BF = jnp.bfloat16
F32 = jnp.float32


def series(values, degree):
    nodes = (np.cos(np.pi * (np.arange(400) + 0.5) / 400) + 1.0) * 0.125
    fitted = np.polynomial.chebyshev.Chebyshev.fit(nodes, values(nodes), degree, domain=[0, 0.25])
    return [float(c) for c in fitted.convert(kind=np.polynomial.Polynomial).coef]


COS_COEF = series(lambda q: np.cos(2 * np.pi * np.sqrt(q)), 7)
SIN_COEF = series(lambda q: np.sin(2 * np.pi * np.sqrt(q)) / np.sqrt(q), 6)


def horner(coefs, q):
    total = jnp.full_like(q, coefs[-1])
    for c in coefs[-2::-1]:
        total = total * q + jnp.float32(c)
    return total


def dft_tables():
    centred = np.arange(S) - S // 2
    product = (centred[:, None] * centred[None, :]) % S
    angles = np.float32(2.0 * math.pi / S) * product.astype(np.float32)
    scale = np.float32(1.0 / math.sqrt(S))
    re = (np.cos(angles) * scale).astype(ml_dtypes.bfloat16).astype(np.float32)
    im = (-np.sin(angles) * scale).astype(ml_dtypes.bfloat16).astype(np.float32)
    return re, im


def right_table():
    re, im = dft_tables()
    norm = np.float32(1.0 / math.sqrt(K))
    table = np.zeros((2 * S, 512), np.float32)
    table[:S, :S] = re.T * norm
    table[S:, :S] = -im.T * norm
    table[:S, 256 : 256 + S] = im.T * norm
    table[S:, 256 : 256 + S] = re.T * norm
    return table


def left_table():
    re, im = dft_tables()
    order = np.concatenate([np.arange(0, S, 2), np.arange(1, S, 2)])
    re, im = re[:, order], im[:, order]
    table = np.zeros((8, 2, ROWS, 2 * S), np.float32)
    for shift in range(8):
        table[shift, 0, shift : shift + S, :S] = re
        table[shift, 0, shift : shift + S, S:] = -im
        table[shift, 1, shift : shift + S, :S] = im
        table[shift, 1, shift : shift + S, S:] = re
    return table.reshape(8, 2 * ROWS, 2 * S).astype(ml_dtypes.bfloat16)


def pack_kernel(head, off_u, off_v, base, pairs, data, track, out_data, out_meta, rows, counts):
    for h in range(5):
        counts[h] = 0
    out_meta[...] = jnp.zeros_like(out_meta)
    lane = lax.broadcasted_iota(jnp.int32, (TB, 128), 1)
    time = lax.broadcasted_iota(jnp.int32, (TB, 128), 0)
    dims = (((0,), (0,)), ((), ()))
    rows[...] = sum(
        lax.dot_general(
            track[a],
            jnp.where(lane == time + 8 * (a + 1), 1.0, 0.0).astype(BF),
            dims,
            preferred_element_type=F32,
        )
        for a in range(2)
    )
    lane = lax.broadcasted_iota(jnp.int32, (1, 128), 1)

    def one(b, carry):
        h = head[b]
        slot = h * CAP + counts[h]
        counts[h] = counts[h] + 1
        out_data[slot] = data[b]
        label = base[b]
        row = jnp.where(lane == 0, 1, 0)
        row = jnp.where(lane == 1, off_u[b], row)
        row = jnp.where(lane == 2, off_v[b], row)
        row = jnp.where(lane == 3, pairs[0, label], row)
        row = jnp.where(lane == 4, pairs[1, label], row)
        out_meta[pl.ds(slot, 1), :] = rows[pl.ds(b, 1), :] + row.astype(F32)
        return carry

    lax.fori_loop(0, B_DEV, one, 0)


def exchange_kernel(data, meta, got_data, got_meta, send_sems, recv_sems):
    au, vert = lax.axis_index("au"), lax.axis_index("vert")
    n_au, n_vert = lax.axis_size("au"), lax.axis_size("vert")
    near = (
        {"au": lax.rem(au + 1, n_au)},
        {"au": lax.rem(au + n_au - 1, n_au)},
        {"vert": lax.rem(vert + 1, n_vert)},
        {"vert": lax.rem(vert + n_vert - 1, n_vert)},
    )
    barrier = pltpu.get_barrier_semaphore()
    for device in near:
        pl.semaphore_signal(barrier, inc=1, device_id=device, device_id_type=MESH)
    pl.semaphore_wait(barrier, 4)
    copies = []
    for i, device in enumerate(near):
        for j, (source, target) in enumerate(((data, got_data), (meta, got_meta))):
            copy = pltpu.make_async_remote_copy(
                src_ref=source.at[pl.ds((i + 1) * CAP, CAP)],
                dst_ref=target.at[pl.ds(i * CAP, CAP)],
                send_sem=send_sems.at[i, j],
                recv_sem=recv_sems.at[i, j],
                device_id=device,
                device_id_type=MESH,
            )
            copy.start()
            copies.append(copy)
    for copy in copies:
        copy.wait()


def swap_halves(x):
    return pltpu.roll(x, S, x.ndim - 1)


def enlist_blocks(own_meta, got_meta, listing):
    def place(slot, read, counts):
        filled = read(0)
        off_u, off_v = read(1), read(2)
        past = jnp.logical_or(off_u > TU - S, off_v > TV - S)
        index = jnp.where(past, counts[0], LATER + counts[1])

        @pl.when(filled == 1)
        def _():
            listing[0, index] = slot
            listing[1, index] = off_u
            listing[2, index] = off_v
            listing[3, index] = read(3)
            listing[4, index] = read(4)

        early = jnp.where(past, filled, 0)
        return counts[0] + early, counts[1] + filled - early

    def one_own(slot, counts):
        return place(slot, lambda c: own_meta[slot, c].astype(jnp.int32), counts)

    def one_got(slot, counts):
        return place(slot + CAP, lambda c: got_meta[slot, c].astype(jnp.int32), counts)

    counts = (jnp.int32(0), jnp.int32(0))
    counts = lax.fori_loop(0, CAP, one_own, counts)
    counts = lax.fori_loop(0, SLOTS - CAP, one_got, counts)
    for start, number in zip((0, LATER), counts):

        @pl.when(number % 2 == 1)
        def _():
            for column in range(5):
                listing[column, start + number] = listing[column, start + number - 1]
            listing[1, start + number] = TU + S

    return (counts[0] + 1) // 2, (counts[1] + 1) // 2


def arrange_station(raw, tall):
    value = raw.astype(F32)
    for i in range(S // 2):
        tall[8 * i : 8 * i + 4, :] = value[:, 128 * i : 128 * (i + 1)]
    lane = lax.broadcasted_iota(jnp.int32, (S // 2, 128), 1)
    feeds = []
    for f in range(2):
        re = tall[pl.ds(2 * f, S // 2, stride=8), :]
        im = tall[pl.ds(2 * f + 1, S // 2, stride=8), :]
        even = jnp.where(lane < S, re, swap_halves(im))
        odd = jnp.where(lane < S, swap_halves(re), im)
        feeds.append(jnp.concatenate([even, odd], axis=0).astype(BF))
    return feeds


def image_kernel(
    own_meta_in, got_meta_in, own_data, got_data, own_screens,
    images, arranged,
    own_meta, got_meta, data, tracks, spread, raw, tall, mult, listing, sems,
):
    meta_copies = [
        pltpu.make_async_copy(own_meta_in.at[:CAP], own_meta, sems.at[1]),
        pltpu.make_async_copy(got_meta_in, got_meta, sems.at[2]),
        pltpu.make_async_copy(own_meta_in.at[:CAP], tracks.at[:CAP], sems.at[3]),
        pltpu.make_async_copy(got_meta_in, tracks.at[CAP:], sems.at[4]),
    ]
    data_copies = [
        pltpu.make_async_copy(own_data.at[:CAP], data.at[:CAP], sems.at[5]),
        pltpu.make_async_copy(got_data, data.at[CAP:], sems.at[6]),
    ]
    for copy in meta_copies + data_copies:
        copy.start()
    fetch = pltpu.make_async_copy(own_screens, raw, sems.at[0])
    fetch.start()
    band = lax.axis_index("ch")
    channels = CH_DEV * lax.axis_size("ch")
    row = lax.broadcasted_iota(jnp.int32, (32, K), 0)
    channel = band * CH_DEV + lax.broadcasted_iota(jnp.int32, (32, K), 1) % CH_DEV
    ratio = 1.0 + channel.astype(F32) / jnp.float32(2 * channels)
    coarse = row - 8
    coarse_u = 16 * (coarse % 4) + coarse // 4 - S // 2
    fine_v = row - 16
    coarse_v = (row - 24) * 8 - S // 2
    step = jnp.where(
        row < 16, jnp.where(row < 8, 2 * row, coarse_u), jnp.where(row < 24, fine_v, coarse_v)
    )
    mult[...] = step.astype(F32) / S * ratio
    for copy in meta_copies:
        copy.wait()
    source = lax.broadcasted_iota(jnp.int32, (128, 2 * K), 0)
    column = lax.broadcasted_iota(jnp.int32, (128, 2 * K), 1)
    chosen = jnp.where(source == 8 + column // CH_DEV, 1.0, 0.0).astype(BF)
    lane = lax.broadcasted_iota(jnp.int32, (SLOTS, 128), 1)
    only = jnp.where(lane < 8, 0.0, tracks[...]).astype(BF)
    spread[...] = jnp.dot(only, chosen, preferred_element_type=F32)
    early, late = enlist_blocks(own_meta, got_meta, listing)
    for copy in data_copies:
        copy.wait()

    def block(index):
        slot = listing[0, index]
        sample = data[slot].astype(F32)
        track = spread[pl.ds(slot, 1), :]
        turns = jnp.concatenate(
            [track[:, :K] * mult[:16], track[:, K:] * mult[16:]], axis=0
        )
        frac = turns - jnp.floor(turns + 0.5)
        square = frac * frac
        cos = horner(COS_COEF, square)
        sin = horner(SIN_COEF, square) * frac

        def phasors(first):
            cos_fine, sin_fine = cos[first : first + 8], sin[first : first + 8]
            all_cos, all_sin = [], []
            for a in range(8):
                at = first + 8 + a
                cos_a, sin_a = cos[at : at + 1], sin[at : at + 1]
                all_cos.append(cos_fine * cos_a - sin_fine * sin_a)
                all_sin.append(sin_fine * cos_a + cos_fine * sin_a)
            return (
                jnp.concatenate(all_cos, axis=0).astype(BF),
                jnp.concatenate(all_sin, axis=0).astype(BF),
            )

        cos_u, sin_u = phasors(0)
        cos_u, sin_u = cos_u.astype(F32), sin_u.astype(F32)
        cos_v, sin_v = phasors(16)
        table_re = jnp.concatenate([cos_v, sin_v], axis=0)
        table_im = jnp.concatenate([-sin_v, cos_v], axis=0)
        weigh_re, weigh_im = [], []
        for p in range(4):
            re, im = sample[2 * p : 2 * p + 1], sample[2 * p + 1 : 2 * p + 2]
            weigh_re.append((re * cos_u - im * sin_u).astype(BF))
            weigh_im.append((re * sin_u + im * cos_u).astype(BF))
        dims = (((1,), (1,)), ((), ()))
        image = lax.dot_general(
            jnp.concatenate(weigh_re, axis=0), table_re, dims, preferred_element_type=F32
        ) + lax.dot_general(
            jnp.concatenate(weigh_im, axis=0), table_im, dims, preferred_element_type=F32
        )
        return image.astype(BF)

    def loop(pair, carry):
        at = jnp.where(pair < early, 2 * pair, LATER + 2 * (pair - early))
        first, second = block(at), block(at + 1)
        images[2 * pair] = first
        images[2 * pair + 1] = second
        return carry

    lax.fori_loop(0, early + late, loop, 0)
    fetch.wait()

    def arrange(pair, carry):
        for i in range(2):
            feeds = arrange_station(raw[2 * pair + i], tall.at[i])
            for f in range(2):
                arranged[2 * pair + i, f] = feeds[f]
        return carry

    lax.fori_loop(0, raw.shape[0] // 2, arrange, 0)


def folded(x):
    middle = x.shape[1] // 2
    lane = lax.broadcasted_iota(jnp.int32, (1, 1, 128), 2)
    return jnp.where(lane < S, x[:, :middle], swap_halves(x[:, middle:])).astype(BF)


def early_kernel(
    own_meta_in, got_meta_in, images, arranged, got_screens, right_in, left_in,
    canvas, screens, edge_u, edge_v, corner,
    own_meta, got_meta, raw, right, left, tall, listing, sems,
):
    here = arranged.shape[0]
    meta_copies = [
        pltpu.make_async_copy(own_meta_in.at[:CAP], own_meta, sems.at[0]),
        pltpu.make_async_copy(got_meta_in, got_meta, sems.at[1]),
    ]
    fetches = [
        pltpu.make_async_copy(got_screens, raw, sems.at[2]),
        pltpu.make_async_copy(arranged, screens.at[:here], sems.at[3]),
        pltpu.make_async_copy(right_in, right, sems.at[4]),
        pltpu.make_async_copy(left_in, left, sems.at[5]),
    ]
    for copy in meta_copies + fetches:
        copy.start()
    canvas[...] = jnp.zeros_like(canvas)
    for copy in meta_copies:
        copy.wait()
    early, _ = enlist_blocks(own_meta, got_meta, listing)
    for copy in fetches:
        copy.wait()

    def arrange(pair, carry):
        for i in range(2):
            feeds = arrange_station(raw[2 * pair + i], tall.at[i])
            for f in range(2):
                screens[here + 2 * pair + i, f] = feeds[f]
        return carry

    lax.fori_loop(0, here // 2, arrange, 0)
    grid_blocks(images, screens, canvas, right, left, listing, early, 0, 0)
    edge_u[...] = canvas[:, TU : TU + S, :TV].astype(BF)
    edge_v[...] = folded(canvas[:, :TU, TV:])
    corner[...] = folded(canvas[:, TU : TU + S, TV:])


def late_kernel(
    own_meta_in, got_meta_in, images, canvas_in, screens, right_in, left_in,
    canvas, tile,
    own_meta, got_meta, right, left, listing, sems,
):
    meta_copies = [
        pltpu.make_async_copy(own_meta_in.at[:CAP], own_meta, sems.at[0]),
        pltpu.make_async_copy(got_meta_in, got_meta, sems.at[1]),
    ]
    fetches = [
        pltpu.make_async_copy(right_in, right, sems.at[2]),
        pltpu.make_async_copy(left_in, left, sems.at[3]),
    ]
    for copy in meta_copies + fetches:
        copy.start()
    for copy in meta_copies:
        copy.wait()
    early, late = enlist_blocks(own_meta, got_meta, listing)
    for copy in fetches:
        copy.wait()
    grid_blocks(images, screens, canvas, right, left, listing, late, LATER, 2 * early)
    store = pltpu.make_async_copy(canvas.at[:, :TU, :TV], tile, sems.at[4])
    store.start()
    store.wait()


def grid_blocks(images, screens, canvas, right, left, listing, pairs, first, first_image):
    here = screens.shape[0] // 2
    band = lax.axis_index("ch")

    def screen_place(station):
        owner = station // here
        local = station - owner * here
        return jnp.where(owner == band, local, here + local)

    def block(number):
        index = first + number
        off_u = listing[1, index]
        off_v = listing[2, index]
        one = screen_place(listing[3, index])
        two = screen_place(listing[4, index])
        two_s = [screens[two, f].astype(F32) for f in range(2)]
        fixed = []
        for f in range(2):
            one_s = screens[one, f].astype(F32)
            one_swapped = swap_halves(one_s)
            for e in range(2):
                p = 2 * f + e
                same = one_s * two_s[e]
                cross = one_swapped * two_s[e]
                gain_re = same + swap_halves(same)
                gain_im = swap_halves(cross) - cross
                part = images[first_image + number, p * S : (p + 1) * S].astype(F32)
                fixed.append((part * gain_re + swap_halves(part) * gain_im).astype(BF))
        lanes = off_v // 128
        shift = off_v - lanes * 128
        shifted = jnp.concatenate(
            [
                pltpu.roll(right[:, :256], shift, 1).astype(BF),
                pltpu.roll(right[:, 256:], shift, 1).astype(BF),
            ],
            axis=1,
        )
        half = jnp.dot(
            jnp.concatenate(fixed, axis=0), shifted, preferred_element_type=F32
        ).astype(BF)
        eighth = off_u // 8
        placed = left[off_u - eighth * 8]
        start_u = pl.multiple_of(eighth * 8, 8)
        start_v = pl.multiple_of(lanes * 128, 128)
        grids = []
        for p in range(4):
            part = half[p * S : (p + 1) * S]
            both = jnp.concatenate([part[:, :256], part[:, 256:]], axis=0)
            grids.append(jnp.dot(placed, both, preferred_element_type=F32))
        return start_u, start_v, grids

    def loop(pair, carry):
        for start_u, start_v, grids in [block(2 * pair), block(2 * pair + 1)]:
            for p in range(4):
                for r in range(2):
                    where = (2 * p + r, pl.ds(start_u, ROWS), pl.ds(start_v, 256))
                    canvas[where] += grids[p][r * ROWS : (r + 1) * ROWS]
        return carry

    lax.fori_loop(0, pairs, loop, 0)


def finish_kernel(tile, canvas, got_u, got_v, got_c, out, top, side, sems):
    lane = lax.broadcasted_iota(jnp.int32, (1, 1, 128), 2)

    def unfolded(x):
        x = x.astype(F32)
        low = jnp.where(lane < S, x, 0.0)
        high = jnp.where(lane < S, swap_halves(x), 0.0)
        return low, high

    low, high = unfolded(got_v[...])
    first, second = unfolded(got_c[...])
    top[...] = canvas[:, :S, :TV] + got_u[...].astype(F32)
    top[:, :, :128] += low[:, :S] + jnp.concatenate([first, second], axis=1)
    store_top = pltpu.make_async_copy(top, out.at[:, :S, :], sems.at[0])
    store_top.start()
    side[:, : TU // 2 - S] = canvas[:, S : TU // 2, :128] + low[:, S:]
    side[:, TU // 2 - S :] = canvas[:, TU // 2 : TU, :128] + high
    store_side = pltpu.make_async_copy(side, out.at[:, S:, :128], sems.at[1])
    store_side.start()
    store_top.wait()
    store_side.wait()


def body(visibilities, tracks, offset_u, offset_v, heading, baseline, station_pair, screens):
    smem = pl.BlockSpec(memory_space=pltpu.SMEM)
    vmem = pl.BlockSpec(memory_space=pltpu.VMEM)
    anywhere = pl.BlockSpec(memory_space=pl.ANY)
    n_ch, n_au, n_vert = (lax.axis_size(axis) for axis in ("ch", "au", "vert"))
    here = screens.shape[0]
    got_screens = lax.ppermute(screens, "ch", [(i, (i + 1) % n_ch) for i in range(n_ch)])

    packed, meta = pl.pallas_call(
        pack_kernel,
        out_shape=(
            jax.ShapeDtypeStruct((SLOTS, 8, K), BF),
            jax.ShapeDtypeStruct((SLOTS, 128), F32),
        ),
        in_specs=[smem] * 5 + [vmem] * 2,
        out_specs=(vmem, vmem),
        scratch_shapes=[pltpu.VMEM((B_DEV, 128), F32), pltpu.SMEM((8,), jnp.int32)],
    )(
        heading[:, 0], offset_u, offset_v, baseline, station_pair, visibilities,
        tracks.transpose(1, 2, 0),
    )
    got_data, got_meta = pl.pallas_call(
        exchange_kernel,
        out_shape=(
            jax.ShapeDtypeStruct((SLOTS - CAP, 8, K), BF),
            jax.ShapeDtypeStruct((SLOTS - CAP, 128), F32),
        ),
        in_specs=[anywhere, anywhere],
        out_specs=(anywhere, anywhere),
        scratch_shapes=[pltpu.SemaphoreType.DMA((4, 2)), pltpu.SemaphoreType.DMA((4, 2))],
        compiler_params=pltpu.CompilerParams(collective_id=0, has_side_effects=True),
    )(packed, meta)
    meta_scratch = [pltpu.SMEM((CAP, 128), F32), pltpu.SMEM((SLOTS - CAP, 128), F32)]
    listing = pltpu.SMEM((8, 2 * LATER), jnp.int32)
    images, arranged = pl.pallas_call(
        image_kernel,
        out_shape=(
            jax.ShapeDtypeStruct((SLOTS + 2, 4 * S, 2 * S), BF),
            jax.ShapeDtypeStruct((here, 2, S, 2 * S), BF),
        ),
        in_specs=[anywhere] * 5,
        out_specs=(vmem, vmem),
        scratch_shapes=meta_scratch
        + [
            pltpu.VMEM((SLOTS, 8, K), BF),
            pltpu.VMEM((SLOTS, 128), F32),
            pltpu.VMEM((SLOTS, 2 * K), F32),
            pltpu.VMEM(screens.shape, BF),
            pltpu.VMEM((2, 4 * S, 128), F32),
            pltpu.VMEM((32, K), F32),
            listing,
            pltpu.SemaphoreType.DMA((7,)),
        ],
        compiler_params=pltpu.CompilerParams(vmem_limit_bytes=12 << 20),
        cost_estimate=pl.CostEstimate(
            flops=SLOTS * 2 * 256 * 512 * 128 * 8, bytes_accessed=8 << 20, transcendentals=0
        ),
    )(meta, got_meta, packed, got_data, screens)
    right, left = jnp.asarray(right_table()), jnp.asarray(left_table())
    table_scratch = [pltpu.VMEM((2 * S, 512), F32), pltpu.VMEM((8, 2 * ROWS, 2 * S), BF)]
    canvas_shape = jax.ShapeDtypeStruct((8, TU + S + ROWS, TV + 128), F32)
    canvas, all_screens, edge_u, edge_v, corner = pl.pallas_call(
        early_kernel,
        out_shape=(
            canvas_shape,
            jax.ShapeDtypeStruct((2 * here, 2, S, 2 * S), BF),
            jax.ShapeDtypeStruct((8, S, TV), BF),
            jax.ShapeDtypeStruct((8, TU // 2, 128), BF),
            jax.ShapeDtypeStruct((8, S // 2, 128), BF),
        ),
        in_specs=[anywhere] * 2 + [vmem] + [anywhere] * 4,
        out_specs=(vmem,) * 5,
        scratch_shapes=meta_scratch
        + [pltpu.VMEM(screens.shape, BF)]
        + table_scratch
        + [pltpu.VMEM((2, 4 * S, 128), F32), listing, pltpu.SemaphoreType.DMA((6,))],
        compiler_params=pltpu.CompilerParams(vmem_limit_bytes=12 << 20),
    )(meta, got_meta, images, arranged, got_screens, right, left)
    got_u = lax.ppermute(edge_u, "au", [(i, (i + 1) % n_au) for i in range(n_au)])
    got_v = lax.ppermute(edge_v, "vert", [(i, (i + 1) % n_vert) for i in range(n_vert)])
    diagonal = [
        (u * n_vert + v, (u + 1) % n_au * n_vert + (v + 1) % n_vert)
        for u in range(n_au)
        for v in range(n_vert)
    ]
    got_c = lax.ppermute(corner, ("au", "vert"), diagonal)
    canvas, tile = pl.pallas_call(
        late_kernel,
        out_shape=(canvas_shape, jax.ShapeDtypeStruct((8, TU, TV), F32)),
        in_specs=[anywhere] * 2 + [vmem] * 3 + [anywhere] * 2,
        out_specs=(vmem, anywhere),
        scratch_shapes=meta_scratch + table_scratch + [listing, pltpu.SemaphoreType.DMA((5,))],
        input_output_aliases={3: 0},
        compiler_params=pltpu.CompilerParams(vmem_limit_bytes=12 << 20),
        cost_estimate=pl.CostEstimate(
            flops=SLOTS * 2 * 256 * 512 * 128 * 8, bytes_accessed=8 << 20, transcendentals=0
        ),
    )(meta, got_meta, images, canvas, all_screens, right, left)
    out = pl.pallas_call(
        finish_kernel,
        out_shape=jax.ShapeDtypeStruct((8, TU, TV), F32),
        in_specs=[anywhere] + [vmem] * 4,
        out_specs=anywhere,
        scratch_shapes=[
            pltpu.VMEM((8, S, TV), F32),
            pltpu.VMEM((8, TU - S, 128), F32),
            pltpu.SemaphoreType.DMA((2,)),
        ],
        input_output_aliases={0: 0},
        compiler_params=pltpu.CompilerParams(vmem_limit_bytes=8 << 20),
    )(tile, canvas, got_u, got_v, got_c)
    return out[None]


def solution(mesh):
    placed = (
        P(("au", "vert"), None, "ch"),
        P(("au", "vert"), None, None),
        P(("au", "vert")),
        P(("au", "vert")),
        P(("au", "vert"), None),
        P(("au", "vert")),
        P(),
        P("ch", None, None),
    )
    return jax.shard_map(
        body, mesh=mesh, in_specs=placed, out_specs=P("ch", None, "au", "vert"), check_vma=False
    )
```

```python
import math

import jax
import jax.numpy as jnp
import ml_dtypes
import numpy as np
from jax import lax
from jax.experimental import pallas as pl
from jax.experimental.pallas import tpu as pltpu
from jax.sharding import PartitionSpec as P

S = 64
CH_DEV = 32
TB = 8
K = TB * CH_DEV
B_DEV = 32
CAP = B_DEV // 4
SLOTS = 5 * CAP
TU = 256
TV = 256
ROWS = 72
LATER = 48
MESH = pl.DeviceIdType.MESH
BF = jnp.bfloat16
F32 = jnp.float32


def series(values, degree):
    nodes = (np.cos(np.pi * (np.arange(400) + 0.5) / 400) + 1.0) * 0.125
    fitted = np.polynomial.chebyshev.Chebyshev.fit(nodes, values(nodes), degree, domain=[0, 0.25])
    return [float(c) for c in fitted.convert(kind=np.polynomial.Polynomial).coef]


COS_COEF = series(lambda q: np.cos(2 * np.pi * np.sqrt(q)), 7)
SIN_COEF = series(lambda q: np.sin(2 * np.pi * np.sqrt(q)) / np.sqrt(q), 6)


def horner(coefs, q):
    total = jnp.full_like(q, coefs[-1])
    for c in coefs[-2::-1]:
        total = total * q + jnp.float32(c)
    return total


def dft_tables():
    centred = np.arange(S) - S // 2
    product = (centred[:, None] * centred[None, :]) % S
    angles = np.float32(2.0 * math.pi / S) * product.astype(np.float32)
    scale = np.float32(1.0 / math.sqrt(S))
    re = (np.cos(angles) * scale).astype(ml_dtypes.bfloat16).astype(np.float32)
    im = (-np.sin(angles) * scale).astype(ml_dtypes.bfloat16).astype(np.float32)
    return re, im


def right_table():
    re, im = dft_tables()
    norm = np.float32(1.0 / math.sqrt(K))
    table = np.zeros((2 * S, 256), np.float32)
    table[:S, :S] = re.T * norm
    table[S:, :S] = im.T * norm
    return table


def left_table():
    re, im = dft_tables()
    order = np.concatenate([np.arange(0, S, 2), np.arange(1, S, 2)])
    re, im = re[:, order], im[:, order]
    table = np.zeros((8, 2, ROWS, 2 * S), np.float32)
    for shift in range(8):
        table[shift, 0, shift : shift + S, :S] = re
        table[shift, 0, shift : shift + S, S:] = -im
        table[shift, 1, shift : shift + S, :S] = im
        table[shift, 1, shift : shift + S, S:] = re
    return table.reshape(8, 2 * ROWS, 2 * S).astype(ml_dtypes.bfloat16)


def pack_kernel(head, off_u, off_v, base, pairs, data, track, out_data, out_meta, rows, counts):
    for h in range(5):
        counts[h] = 0
    out_meta[...] = jnp.zeros_like(out_meta)
    lane = lax.broadcasted_iota(jnp.int32, (TB, 128), 1)
    time = lax.broadcasted_iota(jnp.int32, (TB, 128), 0)
    dims = (((0,), (0,)), ((), ()))
    rows[...] = sum(
        lax.dot_general(
            track[a],
            jnp.where(lane == time + 8 * (a + 1), 1.0, 0.0).astype(BF),
            dims,
            preferred_element_type=F32,
        )
        for a in range(2)
    )
    lane = lax.broadcasted_iota(jnp.int32, (1, 128), 1)

    def one(b, carry):
        h = head[b]
        slot = h * CAP + counts[h]
        counts[h] = counts[h] + 1
        out_data[slot] = data[b]
        label = base[b]
        row = jnp.where(lane == 0, 1, 0)
        row = jnp.where(lane == 1, off_u[b], row)
        row = jnp.where(lane == 2, off_v[b], row)
        row = jnp.where(lane == 3, pairs[0, label], row)
        row = jnp.where(lane == 4, pairs[1, label], row)
        out_meta[pl.ds(slot, 1), :] = rows[pl.ds(b, 1), :] + row.astype(F32)
        return carry

    lax.fori_loop(0, B_DEV, one, 0)


def exchange_kernel(data, meta, got_data, got_meta, send_sems, recv_sems, own_sems):
    au, vert = lax.axis_index("au"), lax.axis_index("vert")
    n_au, n_vert = lax.axis_size("au"), lax.axis_size("vert")
    near = (
        {"au": lax.rem(au + 1, n_au)},
        {"au": lax.rem(au + n_au - 1, n_au)},
        {"vert": lax.rem(vert + 1, n_vert)},
        {"vert": lax.rem(vert + n_vert - 1, n_vert)},
    )
    copies = []
    for j, (source, target) in enumerate(((data, got_data), (meta, got_meta))):
        copy = pltpu.make_async_copy(
            source.at[pl.ds(0, CAP)], target.at[pl.ds(0, CAP)], own_sems.at[j]
        )
        copy.start()
        copies.append(copy)
    barrier = pltpu.get_barrier_semaphore()
    for device in near:
        pl.semaphore_signal(barrier, inc=1, device_id=device, device_id_type=MESH)
    pl.semaphore_wait(barrier, 4)
    for i, device in enumerate(near):
        for j, (source, target) in enumerate(((data, got_data), (meta, got_meta))):
            copy = pltpu.make_async_remote_copy(
                src_ref=source.at[pl.ds((i + 1) * CAP, CAP)],
                dst_ref=target.at[pl.ds((i + 1) * CAP, CAP)],
                send_sem=send_sems.at[i, j],
                recv_sem=recv_sems.at[i, j],
                device_id=device,
                device_id_type=MESH,
            )
            copy.start()
            copies.append(copy)
    for copy in copies:
        copy.wait()


def swap_halves(x):
    return pltpu.roll(x, S, x.ndim - 1)


def enlist_blocks(labels, listing):
    def place(slot, read, counts):
        filled = read(0)
        off_u, off_v = read(1), read(2)
        past = jnp.logical_or(off_u > TU - S, off_v > TV - S)
        index = jnp.where(past, counts[0], LATER + counts[1])

        @pl.when(filled == 1)
        def _():
            listing[0, index] = slot
            listing[1, index] = off_u
            listing[2, index] = off_v
            listing[3, index] = read(3)
            listing[4, index] = read(4)

        early = jnp.where(past, filled, 0)
        return counts[0] + early, counts[1] + filled - early

    def one(slot, counts):
        return place(slot, lambda c: labels[slot, c].astype(jnp.int32), counts)

    counts = lax.fori_loop(0, SLOTS, one, (jnp.int32(0), jnp.int32(0)))
    for start, number in zip((0, LATER), counts):

        @pl.when(number % 2 == 1)
        def _():
            for column in range(5):
                listing[column, start + number] = listing[column, start + number - 1]
            listing[1, start + number] = TU + S

    return (counts[0] + 1) // 2, (counts[1] + 1) // 2


def arrange_station(raw, tall):
    value = raw.astype(F32)
    for i in range(S // 2):
        tall[8 * i : 8 * i + 4, :] = value[:, 128 * i : 128 * (i + 1)]
    lane = lax.broadcasted_iota(jnp.int32, (S // 2, 128), 1)
    feeds = []
    for f in range(2):
        re = tall[pl.ds(2 * f, S // 2, stride=8), :]
        im = tall[pl.ds(2 * f + 1, S // 2, stride=8), :]
        even = jnp.where(lane < S, re, swap_halves(im))
        odd = jnp.where(lane < S, swap_halves(re), im)
        feeds.append(jnp.concatenate([even, odd], axis=0).astype(BF))
    return feeds


def image_kernel(meta, data, images, labels, spread, mult, listing, sems):
    copy = pltpu.make_async_copy(meta, labels, sems.at[0])
    copy.start()
    band = lax.axis_index("ch")
    channels = CH_DEV * lax.axis_size("ch")
    row = lax.broadcasted_iota(jnp.int32, (32, K), 0)
    channel = band * CH_DEV + lax.broadcasted_iota(jnp.int32, (32, K), 1) % CH_DEV
    ratio = 1.0 + channel.astype(F32) / jnp.float32(2 * channels)
    coarse = row - 8
    coarse_u = 16 * (coarse % 4) + coarse // 4 - S // 2
    fine_v = row - 16
    coarse_v = (row - 24) * 8 - S // 2
    step = jnp.where(
        row < 16, jnp.where(row < 8, 2 * row, coarse_u), jnp.where(row < 24, fine_v, coarse_v)
    )
    mult[...] = step.astype(F32) / S * ratio
    source = lax.broadcasted_iota(jnp.int32, (128, 2 * K), 0)
    column = lax.broadcasted_iota(jnp.int32, (128, 2 * K), 1)
    chosen = jnp.where(source == 8 + column // CH_DEV, 1.0, 0.0).astype(BF)
    lane = lax.broadcasted_iota(jnp.int32, (SLOTS, 128), 1)
    only = jnp.where(lane < 8, 0.0, meta[...]).astype(BF)
    spread[...] = jnp.dot(only, chosen, preferred_element_type=F32)
    copy.wait()
    early, late = enlist_blocks(labels, listing)

    def block(index):
        slot = listing[0, index]
        sample = data[slot].astype(F32)
        track = spread[pl.ds(slot, 1), :]
        turns = jnp.concatenate(
            [track[:, :K] * mult[:16], track[:, K:] * mult[16:]], axis=0
        )
        frac = turns - jnp.floor(turns + 0.5)
        square = frac * frac
        cos = horner(COS_COEF, square)
        sin = horner(SIN_COEF, square) * frac

        def phasors(first):
            cos_fine, sin_fine = cos[first : first + 8], sin[first : first + 8]
            all_cos, all_sin = [], []
            for a in range(8):
                at = first + 8 + a
                cos_a, sin_a = cos[at : at + 1], sin[at : at + 1]
                all_cos.append(cos_fine * cos_a - sin_fine * sin_a)
                all_sin.append(sin_fine * cos_a + cos_fine * sin_a)
            return (
                jnp.concatenate(all_cos, axis=0).astype(BF),
                jnp.concatenate(all_sin, axis=0).astype(BF),
            )

        cos_u, sin_u = phasors(0)
        cos_u, sin_u = cos_u.astype(F32), sin_u.astype(F32)
        cos_v, sin_v = phasors(16)
        table_re = jnp.concatenate([cos_v, sin_v], axis=0)
        table_im = jnp.concatenate([-sin_v, cos_v], axis=0)
        weigh_re, weigh_im = [], []
        for p in range(4):
            re, im = sample[2 * p : 2 * p + 1], sample[2 * p + 1 : 2 * p + 2]
            weigh_re.append((re * cos_u - im * sin_u).astype(BF))
            weigh_im.append((re * sin_u + im * cos_u).astype(BF))
        dims = (((1,), (1,)), ((), ()))
        image = lax.dot_general(
            jnp.concatenate(weigh_re, axis=0), table_re, dims, preferred_element_type=F32
        ) + lax.dot_general(
            jnp.concatenate(weigh_im, axis=0), table_im, dims, preferred_element_type=F32
        )
        return image.astype(BF)

    def loop(pair, carry):
        at = jnp.where(pair < early, 2 * pair, LATER + 2 * (pair - early))
        first, second = block(at), block(at + 1)
        images[2 * pair] = first
        images[2 * pair + 1] = second
        return carry

    lax.fori_loop(0, early + late, loop, 0)


def folded(x):
    middle = x.shape[1] // 2
    lane = lax.broadcasted_iota(jnp.int32, (1, 1, 128), 2)
    return jnp.where(lane < S, x[:, :middle], swap_halves(x[:, middle:])).astype(BF)


def early_kernel(
    meta, images, own_screens, got_screens, right_in, left_in,
    canvas, screens, edge_u, edge_v, corner,
    labels, raw, right, left, tall, listing, sems,
):
    here = own_screens.shape[0]
    meta_copies = [pltpu.make_async_copy(meta, labels, sems.at[0])]
    fetches = [
        pltpu.make_async_copy(own_screens, raw.at[:here], sems.at[2]),
        pltpu.make_async_copy(got_screens, raw.at[here:], sems.at[3]),
        pltpu.make_async_copy(left_in, left, sems.at[4]),
        pltpu.make_async_copy(right_in, right, sems.at[5]),
    ]
    for copy in meta_copies + fetches:
        copy.start()
    canvas[...] = jnp.zeros_like(canvas)
    for copy in meta_copies:
        copy.wait()
    early, _ = enlist_blocks(labels, listing)
    for copy in fetches:
        copy.wait()

    def arrange(pair, carry):
        for i in range(2):
            feeds = arrange_station(raw[2 * pair + i], tall.at[i])
            for f in range(2):
                screens[2 * pair + i, f] = feeds[f]
        return carry

    lax.fori_loop(0, here, arrange, 0)
    grid_blocks(images, screens, canvas, right, left, listing, early, 0, 0)
    edge_u[...] = canvas[:, TU : TU + S, :TV].astype(BF)
    edge_v[...] = folded(canvas[:, :TU, TV:])
    corner[...] = folded(canvas[:, TU : TU + S, TV:])


def late_kernel(
    meta, images, canvas_in, screens, right_in, left_in,
    canvas, tile,
    labels, right, left, listing, sems,
):
    meta_copies = [pltpu.make_async_copy(meta, labels, sems.at[0])]
    fetches = [
        pltpu.make_async_copy(left_in, left, sems.at[2]),
        pltpu.make_async_copy(right_in, right, sems.at[3]),
    ]
    for copy in meta_copies + fetches:
        copy.start()
    for copy in meta_copies:
        copy.wait()
    early, late = enlist_blocks(labels, listing)
    for copy in fetches:
        copy.wait()
    grid_blocks(
        images, screens, canvas, right, left, listing, late, LATER, 2 * early
    )
    store = pltpu.make_async_copy(canvas.at[:, :TU, :TV], tile, sems.at[4])
    store.start()
    store.wait()


def grid_blocks(
    images, screens, canvas, right, left, listing, pairs, first, first_image
):
    here = screens.shape[0] // 2
    band = lax.axis_index("ch")

    def screen_place(station):
        owner = station // here
        local = station - owner * here
        return jnp.where(owner == band, local, here + local)

    def block(number):
        index = first + number
        off_u = listing[1, index]
        off_v = listing[2, index]
        one = screen_place(listing[3, index])
        two = screen_place(listing[4, index])
        two_s = [screens[two, f].astype(F32) for f in range(2)]
        fixed = []
        for f in range(2):
            one_s = screens[one, f].astype(F32)
            one_swapped = swap_halves(one_s)
            for e in range(2):
                p = 2 * f + e
                same = one_s * two_s[e]
                cross = one_swapped * two_s[e]
                gain_re = same + swap_halves(same)
                gain_im = swap_halves(cross) - cross
                part = images[first_image + number, p * S : (p + 1) * S].astype(F32)
                fixed.append((part * gain_re + swap_halves(part) * gain_im).astype(BF))
        lanes = off_v // 128
        moved = pltpu.roll(right[...], off_v - lanes * 128, 1).astype(BF)
        table_re, table_im = moved[:S], moved[S:]
        shifted = jnp.concatenate(
            [
                jnp.concatenate([table_re, -table_im], axis=0),
                jnp.concatenate([table_im, table_re], axis=0),
            ],
            axis=1,
        )
        half = jnp.dot(
            jnp.concatenate(fixed, axis=0), shifted, preferred_element_type=F32
        ).astype(BF)
        eighth = off_u // 8
        placed = left[off_u - eighth * 8]
        start_u = pl.multiple_of(eighth * 8, 8)
        start_v = pl.multiple_of(lanes * 128, 128)
        return start_u, start_v, placed, half

    def loop(pair, carry):
        ready = [block(2 * pair), block(2 * pair + 1)]
        for start_u, start_v, placed, half in ready:
            for p in range(4):
                part = half[p * S : (p + 1) * S]
                both = jnp.concatenate([part[:, :256], part[:, 256:]], axis=0)
                grid = jnp.dot(placed, both, preferred_element_type=F32)
                for r in range(2):
                    where = (2 * p + r, pl.ds(start_u, ROWS), pl.ds(start_v, 256))
                    canvas[where] += grid[r * ROWS : (r + 1) * ROWS]
        return carry

    lax.fori_loop(0, pairs, loop, 0)


def finish_kernel(tile, canvas, got_u, got_v, got_c, out, top, side, sems):
    lane = lax.broadcasted_iota(jnp.int32, (1, 1, 128), 2)

    def unfolded(x):
        x = x.astype(F32)
        low = jnp.where(lane < S, x, 0.0)
        high = jnp.where(lane < S, swap_halves(x), 0.0)
        return low, high

    low, high = unfolded(got_v[...])
    first, second = unfolded(got_c[...])
    top[...] = canvas[:, :S, :TV] + got_u[...].astype(F32)
    top[:, :, :128] += low[:, :S] + jnp.concatenate([first, second], axis=1)
    store_top = pltpu.make_async_copy(top, out.at[:, :S, :], sems.at[0])
    store_top.start()
    side[:, : TU // 2 - S] = canvas[:, S : TU // 2, :128] + low[:, S:]
    side[:, TU // 2 - S :] = canvas[:, TU // 2 : TU, :128] + high
    store_side = pltpu.make_async_copy(side, out.at[:, S:, :128], sems.at[1])
    store_side.start()
    store_top.wait()
    store_side.wait()


def body(visibilities, tracks, offset_u, offset_v, heading, baseline, station_pair, screens):
    smem = pl.BlockSpec(memory_space=pltpu.SMEM)
    vmem = pl.BlockSpec(memory_space=pltpu.VMEM)
    anywhere = pl.BlockSpec(memory_space=pl.ANY)
    n_ch, n_au, n_vert = (lax.axis_size(axis) for axis in ("ch", "au", "vert"))
    here = screens.shape[0]
    got_screens = lax.ppermute(screens, "ch", [(i, (i + 1) % n_ch) for i in range(n_ch)])

    packed, meta = pl.pallas_call(
        pack_kernel,
        out_shape=(
            jax.ShapeDtypeStruct((SLOTS, 8, K), BF),
            jax.ShapeDtypeStruct((SLOTS, 128), F32),
        ),
        in_specs=[smem] * 5 + [vmem] * 2,
        out_specs=(vmem, vmem),
        scratch_shapes=[pltpu.VMEM((B_DEV, 128), F32), pltpu.SMEM((8,), jnp.int32)],
    )(
        heading[:, 0], offset_u, offset_v, baseline, station_pair, visibilities,
        tracks.transpose(1, 2, 0),
    )
    got_data, got_meta = pl.pallas_call(
        exchange_kernel,
        out_shape=(
            jax.ShapeDtypeStruct((SLOTS, 8, K), BF),
            jax.ShapeDtypeStruct((SLOTS, 128), F32),
        ),
        in_specs=[anywhere, anywhere],
        out_specs=(anywhere, anywhere),
        scratch_shapes=[
            pltpu.SemaphoreType.DMA((4, 2)),
            pltpu.SemaphoreType.DMA((4, 2)),
            pltpu.SemaphoreType.DMA((2,)),
        ],
        compiler_params=pltpu.CompilerParams(collective_id=0, has_side_effects=True),
    )(packed, meta)
    labels = [pltpu.SMEM((SLOTS, 128), F32)]
    listing = pltpu.SMEM((8, 2 * LATER), jnp.int32)
    images = pl.pallas_call(
        image_kernel,
        out_shape=jax.ShapeDtypeStruct((SLOTS + 2, 4 * S, 2 * S), BF),
        in_specs=[vmem, vmem],
        out_specs=vmem,
        scratch_shapes=labels
        + [
            pltpu.VMEM((SLOTS, 2 * K), F32),
            pltpu.VMEM((32, K), F32),
            listing,
            pltpu.SemaphoreType.DMA((1,)),
        ],
        compiler_params=pltpu.CompilerParams(vmem_limit_bytes=12 << 20),
        cost_estimate=pl.CostEstimate(
            flops=SLOTS * 2 * 256 * 512 * 128 * 8, bytes_accessed=8 << 20, transcendentals=0
        ),
    )(got_meta, got_data)
    right, left = jnp.asarray(right_table()), jnp.asarray(left_table())
    table_scratch = [pltpu.VMEM((2 * S, 256), F32), pltpu.VMEM((8, 2 * ROWS, 2 * S), BF)]
    canvas_shape = jax.ShapeDtypeStruct((8, TU + S + ROWS, TV + 128), F32)
    canvas, all_screens, edge_u, edge_v, corner = pl.pallas_call(
        early_kernel,
        out_shape=(
            canvas_shape,
            jax.ShapeDtypeStruct((2 * here, 2, S, 2 * S), BF),
            jax.ShapeDtypeStruct((8, S, TV), BF),
            jax.ShapeDtypeStruct((8, TU // 2, 128), BF),
            jax.ShapeDtypeStruct((8, S // 2, 128), BF),
        ),
        in_specs=[anywhere, vmem] + [anywhere] * 4,
        out_specs=(vmem,) * 5,
        scratch_shapes=labels
        + [pltpu.VMEM((2 * here, 4, S * S), BF)]
        + table_scratch
        + [pltpu.VMEM((2, 4 * S, 128), F32), listing, pltpu.SemaphoreType.DMA((6,))],
        compiler_params=pltpu.CompilerParams(vmem_limit_bytes=12 << 20),
    )(got_meta, images, screens, got_screens, right, left)
    got_u = lax.ppermute(edge_u, "au", [(i, (i + 1) % n_au) for i in range(n_au)])
    got_v = lax.ppermute(edge_v, "vert", [(i, (i + 1) % n_vert) for i in range(n_vert)])
    diagonal = [
        (u * n_vert + v, (u + 1) % n_au * n_vert + (v + 1) % n_vert)
        for u in range(n_au)
        for v in range(n_vert)
    ]
    got_c = lax.ppermute(corner, ("au", "vert"), diagonal)
    canvas, tile = pl.pallas_call(
        late_kernel,
        out_shape=(canvas_shape, jax.ShapeDtypeStruct((8, TU, TV), F32)),
        in_specs=[anywhere] + [vmem] * 3 + [anywhere] * 2,
        out_specs=(vmem, anywhere),
        scratch_shapes=labels + table_scratch + [listing, pltpu.SemaphoreType.DMA((6,))],
        input_output_aliases={2: 0},
        compiler_params=pltpu.CompilerParams(vmem_limit_bytes=12 << 20),
        cost_estimate=pl.CostEstimate(
            flops=SLOTS * 2 * 256 * 512 * 128 * 8, bytes_accessed=8 << 20, transcendentals=0
        ),
    )(got_meta, images, canvas, all_screens, right, left)
    out = pl.pallas_call(
        finish_kernel,
        out_shape=jax.ShapeDtypeStruct((8, TU, TV), F32),
        in_specs=[anywhere] + [vmem] * 4,
        out_specs=anywhere,
        scratch_shapes=[
            pltpu.VMEM((8, S, TV), F32),
            pltpu.VMEM((8, TU - S, 128), F32),
            pltpu.SemaphoreType.DMA((2,)),
        ],
        input_output_aliases={0: 0},
        compiler_params=pltpu.CompilerParams(vmem_limit_bytes=8 << 20),
    )(tile, canvas, got_u, got_v, got_c)
    return out[None]


def solution(mesh):
    placed = (
        P(("au", "vert"), None, "ch"),
        P(("au", "vert"), None, None),
        P(("au", "vert")),
        P(("au", "vert")),
        P(("au", "vert"), None),
        P(("au", "vert")),
        P(),
        P("ch", None, None),
    )
    return jax.shard_map(
        body, mesh=mesh, in_specs=placed, out_specs=P("ch", None, "au", "vert"), check_vma=False
    )
```

```python
import math

import jax
import jax.numpy as jnp
import ml_dtypes
import numpy as np
from jax import lax
from jax.experimental import pallas as pl
from jax.experimental.pallas import tpu as pltpu
from jax.sharding import PartitionSpec as P

S = 64
CH_DEV = 32
TB = 8
K = TB * CH_DEV
B_DEV = 32
CAP = B_DEV // 4
SLOTS = 5 * CAP
TU = 256
TV = 256
ROWS = 72
LATER = 48
MESH = pl.DeviceIdType.MESH
BF = jnp.bfloat16
F32 = jnp.float32


def series(values, degree):
    nodes = (np.cos(np.pi * (np.arange(400) + 0.5) / 400) + 1.0) * 0.125
    fitted = np.polynomial.chebyshev.Chebyshev.fit(nodes, values(nodes), degree, domain=[0, 0.25])
    return [float(c) for c in fitted.convert(kind=np.polynomial.Polynomial).coef]


COS_COEF = series(lambda q: np.cos(2 * np.pi * np.sqrt(q)), 7)
SIN_COEF = series(lambda q: np.sin(2 * np.pi * np.sqrt(q)) / np.sqrt(q), 6)


def horner(coefs, q):
    total = jnp.full_like(q, coefs[-1])
    for c in coefs[-2::-1]:
        total = total * q + jnp.float32(c)
    return total


def dft_tables():
    centred = np.arange(S) - S // 2
    product = (centred[:, None] * centred[None, :]) % S
    angles = np.float32(2.0 * math.pi / S) * product.astype(np.float32)
    scale = np.float32(1.0 / math.sqrt(S))
    re = (np.cos(angles) * scale).astype(ml_dtypes.bfloat16).astype(np.float32)
    im = (-np.sin(angles) * scale).astype(ml_dtypes.bfloat16).astype(np.float32)
    return re, im


def right_table():
    re, im = dft_tables()
    norm = np.float32(1.0 / math.sqrt(K))
    table = np.zeros((2 * S, 256), np.float32)
    table[:S, :S] = re.T * norm
    table[S:, :S] = im.T * norm
    return table


def left_table():
    re, im = dft_tables()
    order = np.concatenate([np.arange(0, S, 2), np.arange(1, S, 2)])
    re, im = re[:, order], im[:, order]
    table = np.zeros((8, 2, ROWS, 2 * S), np.float32)
    for shift in range(8):
        table[shift, 0, shift : shift + S, :S] = re
        table[shift, 0, shift : shift + S, S:] = -im
        table[shift, 1, shift : shift + S, :S] = im
        table[shift, 1, shift : shift + S, S:] = re
    return table.reshape(8, 2 * ROWS, 2 * S).astype(ml_dtypes.bfloat16)


def pack_kernel(head, off_u, off_v, base, pairs, data, track, out_data, out_meta, rows, counts):
    for h in range(5):
        counts[h] = 0
    out_meta[...] = jnp.zeros_like(out_meta)
    lane = lax.broadcasted_iota(jnp.int32, (TB, 128), 1)
    time = lax.broadcasted_iota(jnp.int32, (TB, 128), 0)
    dims = (((0,), (0,)), ((), ()))
    rows[...] = sum(
        lax.dot_general(
            track[a],
            jnp.where(lane == time + 8 * (a + 1), 1.0, 0.0).astype(BF),
            dims,
            preferred_element_type=F32,
        )
        for a in range(2)
    )
    lane = lax.broadcasted_iota(jnp.int32, (1, 128), 1)

    def one(b, carry):
        h = head[b]
        slot = h * CAP + counts[h]
        counts[h] = counts[h] + 1
        out_data[slot] = data[b]
        label = base[b]
        row = jnp.where(lane == 0, 1, 0)
        row = jnp.where(lane == 1, off_u[b], row)
        row = jnp.where(lane == 2, off_v[b], row)
        row = jnp.where(lane == 3, pairs[0, label], row)
        row = jnp.where(lane == 4, pairs[1, label], row)
        out_meta[pl.ds(slot, 1), :] = rows[pl.ds(b, 1), :] + row.astype(F32)
        return carry

    lax.fori_loop(0, B_DEV, one, 0)


def exchange_kernel(data, meta, got_data, got_meta, send_sems, recv_sems, own_sems):
    au, vert = lax.axis_index("au"), lax.axis_index("vert")
    n_au, n_vert = lax.axis_size("au"), lax.axis_size("vert")
    near = (
        {"au": lax.rem(au + 1, n_au)},
        {"au": lax.rem(au + n_au - 1, n_au)},
        {"vert": lax.rem(vert + 1, n_vert)},
        {"vert": lax.rem(vert + n_vert - 1, n_vert)},
    )
    copies = []
    for j, (source, target) in enumerate(((data, got_data), (meta, got_meta))):
        copy = pltpu.make_async_copy(
            source.at[pl.ds(0, CAP)], target.at[pl.ds(0, CAP)], own_sems.at[j]
        )
        copy.start()
        copies.append(copy)
    barrier = pltpu.get_barrier_semaphore()
    for device in near:
        pl.semaphore_signal(barrier, inc=1, device_id=device, device_id_type=MESH)
    pl.semaphore_wait(barrier, 4)
    for i, device in enumerate(near):
        for j, (source, target) in enumerate(((data, got_data), (meta, got_meta))):
            copy = pltpu.make_async_remote_copy(
                src_ref=source.at[pl.ds((i + 1) * CAP, CAP)],
                dst_ref=target.at[pl.ds((i + 1) * CAP, CAP)],
                send_sem=send_sems.at[i, j],
                recv_sem=recv_sems.at[i, j],
                device_id=device,
                device_id_type=MESH,
            )
            copy.start()
            copies.append(copy)
    for copy in copies:
        copy.wait()


def swap_halves(x):
    return pltpu.roll(x, S, x.ndim - 1)


def enlist_blocks(labels, listing):
    def place(slot, read, counts):
        filled = read(0)
        off_u, off_v = read(1), read(2)
        past = jnp.logical_or(off_u > TU - S, off_v > TV - S)
        index = jnp.where(past, counts[0], LATER + counts[1])

        @pl.when(filled == 1)
        def _():
            listing[0, index] = slot
            listing[1, index] = off_u
            listing[2, index] = off_v
            listing[3, index] = read(3)
            listing[4, index] = read(4)

        early = jnp.where(past, filled, 0)
        return counts[0] + early, counts[1] + filled - early

    def one(slot, counts):
        return place(slot, lambda c: labels[slot, c].astype(jnp.int32), counts)

    counts = lax.fori_loop(0, SLOTS, one, (jnp.int32(0), jnp.int32(0)))
    for start, number in zip((0, LATER), counts):

        @pl.when(number % 2 == 1)
        def _():
            for column in range(5):
                listing[column, start + number] = listing[column, start + number - 1]
            listing[1, start + number] = TU + S

    return (counts[0] + 1) // 2, (counts[1] + 1) // 2


def arrange_station(raw, tall):
    value = raw.astype(F32)
    for i in range(S // 2):
        tall[8 * i : 8 * i + 4, :] = value[:, 128 * i : 128 * (i + 1)]
    lane = lax.broadcasted_iota(jnp.int32, (S // 2, 128), 1)
    feeds = []
    for f in range(2):
        re = tall[pl.ds(2 * f, S // 2, stride=8), :]
        im = tall[pl.ds(2 * f + 1, S // 2, stride=8), :]
        even = jnp.where(lane < S, re, swap_halves(im))
        odd = jnp.where(lane < S, swap_halves(re), im)
        feeds.append(jnp.concatenate([even, odd], axis=0).astype(BF))
    return feeds


def image_kernel(meta, data, images, labels, spread, mult, listing, sems):
    copy = pltpu.make_async_copy(meta, labels, sems.at[0])
    copy.start()
    band = lax.axis_index("ch")
    channels = CH_DEV * lax.axis_size("ch")
    row = lax.broadcasted_iota(jnp.int32, (32, K), 0)
    channel = band * CH_DEV + lax.broadcasted_iota(jnp.int32, (32, K), 1) % CH_DEV
    ratio = 1.0 + channel.astype(F32) / jnp.float32(2 * channels)
    coarse = row - 8
    coarse_u = 16 * (coarse % 4) + coarse // 4 - S // 2
    fine_v = row - 16
    coarse_v = (row - 24) * 8 - S // 2
    step = jnp.where(
        row < 16, jnp.where(row < 8, 2 * row, coarse_u), jnp.where(row < 24, fine_v, coarse_v)
    )
    mult[...] = step.astype(F32) / S * ratio
    source = lax.broadcasted_iota(jnp.int32, (128, 2 * K), 0)
    column = lax.broadcasted_iota(jnp.int32, (128, 2 * K), 1)
    chosen = jnp.where(source == 8 + column // CH_DEV, 1.0, 0.0).astype(BF)
    lane = lax.broadcasted_iota(jnp.int32, (SLOTS, 128), 1)
    only = jnp.where(lane < 8, 0.0, meta[...]).astype(BF)
    spread[...] = jnp.dot(only, chosen, preferred_element_type=F32)
    copy.wait()
    early, late = enlist_blocks(labels, listing)

    def block(index):
        slot = listing[0, index]
        sample = data[slot].astype(F32)
        track = spread[pl.ds(slot, 1), :]
        turns = jnp.concatenate(
            [track[:, :K] * mult[:16], track[:, K:] * mult[16:]], axis=0
        )
        frac = turns - jnp.floor(turns + 0.5)
        square = frac * frac
        cos = horner(COS_COEF, square)
        sin = horner(SIN_COEF, square) * frac

        def phasors(first):
            cos_fine, sin_fine = cos[first : first + 8], sin[first : first + 8]
            all_cos, all_sin = [], []
            for a in range(8):
                at = first + 8 + a
                cos_a, sin_a = cos[at : at + 1], sin[at : at + 1]
                all_cos.append(cos_fine * cos_a - sin_fine * sin_a)
                all_sin.append(sin_fine * cos_a + cos_fine * sin_a)
            return (
                jnp.concatenate(all_cos, axis=0).astype(BF),
                jnp.concatenate(all_sin, axis=0).astype(BF),
            )

        cos_u, sin_u = phasors(0)
        cos_u, sin_u = cos_u.astype(F32), sin_u.astype(F32)
        cos_v, sin_v = phasors(16)
        table_re = jnp.concatenate([cos_v, sin_v], axis=0)
        table_im = jnp.concatenate([-sin_v, cos_v], axis=0)
        weigh_re, weigh_im = [], []
        for p in range(4):
            re, im = sample[2 * p : 2 * p + 1], sample[2 * p + 1 : 2 * p + 2]
            weigh_re.append((re * cos_u - im * sin_u).astype(BF))
            weigh_im.append((re * sin_u + im * cos_u).astype(BF))
        dims = (((1,), (1,)), ((), ()))
        image = lax.dot_general(
            jnp.concatenate(weigh_re, axis=0), table_re, dims, preferred_element_type=F32
        ) + lax.dot_general(
            jnp.concatenate(weigh_im, axis=0), table_im, dims, preferred_element_type=F32
        )
        return image.astype(BF)

    def loop(pair, carry):
        at = jnp.where(pair < early, 2 * pair, LATER + 2 * (pair - early))
        first, second = block(at), block(at + 1)
        images[2 * pair] = first
        images[2 * pair + 1] = second
        return carry

    lax.fori_loop(0, early + late, loop, 0)


def folded(x):
    middle = x.shape[1] // 2
    lane = lax.broadcasted_iota(jnp.int32, (1, 1, 128), 2)
    return jnp.where(lane < S, x[:, :middle], swap_halves(x[:, middle:])).astype(BF)


def early_kernel(
    meta, images, own_screens, near_half, far_half, right_in, left_in,
    canvas, screens, edge_u, edge_v, corner,
    labels, raw, right, left, tall, listing, sems,
):
    here = own_screens.shape[0]
    meta_copies = [pltpu.make_async_copy(meta, labels, sems.at[0])]
    fetches = [
        pltpu.make_async_copy(own_screens, raw.at[:here], sems.at[2]),
        pltpu.make_async_copy(near_half, raw.at[here : here + here // 2], sems.at[3]),
        pltpu.make_async_copy(far_half, raw.at[here + here // 2 :], sems.at[1]),
        pltpu.make_async_copy(left_in, left, sems.at[4]),
        pltpu.make_async_copy(right_in, right, sems.at[5]),
    ]
    for copy in meta_copies + fetches:
        copy.start()
    canvas[...] = jnp.zeros_like(canvas)
    for copy in meta_copies:
        copy.wait()
    early, _ = enlist_blocks(labels, listing)
    for copy in fetches:
        copy.wait()

    def arrange(pair, carry):
        for i in range(2):
            feeds = arrange_station(raw[2 * pair + i], tall.at[i])
            for f in range(2):
                screens[2 * pair + i, f] = feeds[f]
        return carry

    lax.fori_loop(0, here, arrange, 0)
    grid_blocks(images, screens, canvas, right, left, listing, early, 0, 0)
    edge_u[...] = canvas[:, TU : TU + S, :TV].astype(BF)
    edge_v[...] = folded(canvas[:, :TU, TV:])
    corner[...] = folded(canvas[:, TU : TU + S, TV:])


def late_kernel(
    meta, images, canvas_in, screens, right_in, left_in,
    canvas, tile,
    labels, right, left, listing, sems,
):
    meta_copies = [pltpu.make_async_copy(meta, labels, sems.at[0])]
    fetches = [
        pltpu.make_async_copy(left_in, left, sems.at[2]),
        pltpu.make_async_copy(right_in, right, sems.at[3]),
    ]
    for copy in meta_copies + fetches:
        copy.start()
    for copy in meta_copies:
        copy.wait()
    early, late = enlist_blocks(labels, listing)
    for copy in fetches:
        copy.wait()
    grid_blocks(
        images, screens, canvas, right, left, listing, late, LATER, 2 * early
    )
    store = pltpu.make_async_copy(canvas.at[:, :TU, :TV], tile, sems.at[4])
    store.start()
    store.wait()


def grid_blocks(
    images, screens, canvas, right, left, listing, pairs, first, first_image
):
    here = screens.shape[0] // 2
    band = lax.axis_index("ch")
    parity = lax.rem(lax.axis_index("vert"), 2)

    def screen_place(station):
        owner = station // here
        local = station - owner * here
        part = here // 2
        half_of = local // part
        moved = here + local - half_of * part + jnp.where(half_of == parity, 0, part)
        return jnp.where(owner == band, local, moved)

    def block(number):
        index = first + number
        off_u = listing[1, index]
        off_v = listing[2, index]
        one = screen_place(listing[3, index])
        two = screen_place(listing[4, index])
        two_s = [screens[two, f].astype(F32) for f in range(2)]
        fixed = []
        for f in range(2):
            one_s = screens[one, f].astype(F32)
            one_swapped = swap_halves(one_s)
            for e in range(2):
                p = 2 * f + e
                same = one_s * two_s[e]
                cross = one_swapped * two_s[e]
                gain_re = same + swap_halves(same)
                gain_im = swap_halves(cross) - cross
                part = images[first_image + number, p * S : (p + 1) * S].astype(F32)
                fixed.append((part * gain_re + swap_halves(part) * gain_im).astype(BF))
        lanes = off_v // 128
        moved = pltpu.roll(right[...], off_v - lanes * 128, 1).astype(BF)
        table_re, table_im = moved[:S], moved[S:]
        shifted = jnp.concatenate(
            [
                jnp.concatenate([table_re, -table_im], axis=0),
                jnp.concatenate([table_im, table_re], axis=0),
            ],
            axis=1,
        )
        half = jnp.dot(
            jnp.concatenate(fixed, axis=0), shifted, preferred_element_type=F32
        ).astype(BF)
        eighth = off_u // 8
        placed = left[off_u - eighth * 8]
        start_u = pl.multiple_of(eighth * 8, 8)
        start_v = pl.multiple_of(lanes * 128, 128)
        return start_u, start_v, placed, half

    def loop(pair, carry):
        ready = [block(2 * pair), block(2 * pair + 1)]
        for start_u, start_v, placed, half in ready:
            for p in range(4):
                part = half[p * S : (p + 1) * S]
                both = jnp.concatenate([part[:, :256], part[:, 256:]], axis=0)
                grid = jnp.dot(placed, both, preferred_element_type=F32)
                for r in range(2):
                    where = (2 * p + r, pl.ds(start_u, ROWS), pl.ds(start_v, 256))
                    canvas[where] += grid[r * ROWS : (r + 1) * ROWS]
        return carry

    lax.fori_loop(0, pairs, loop, 0)


def finish_kernel(tile, canvas, got_u, got_v, got_c, out, top, side, sems):
    lane = lax.broadcasted_iota(jnp.int32, (1, 1, 128), 2)

    def unfolded(x):
        x = x.astype(F32)
        low = jnp.where(lane < S, x, 0.0)
        high = jnp.where(lane < S, swap_halves(x), 0.0)
        return low, high

    low, high = unfolded(got_v[...])
    first, second = unfolded(got_c[...])
    top[...] = canvas[:, :S, :TV] + got_u[...].astype(F32)
    top[:, :, :128] += low[:, :S] + jnp.concatenate([first, second], axis=1)
    store_top = pltpu.make_async_copy(top, out.at[:, :S, :], sems.at[0])
    store_top.start()
    side[:, : TU // 2 - S] = canvas[:, S : TU // 2, :128] + low[:, S:]
    side[:, TU // 2 - S :] = canvas[:, TU // 2 : TU, :128] + high
    store_side = pltpu.make_async_copy(side, out.at[:, S:, :128], sems.at[1])
    store_side.start()
    store_top.wait()
    store_side.wait()


def body(visibilities, tracks, offset_u, offset_v, heading, baseline, station_pair, screens):
    smem = pl.BlockSpec(memory_space=pltpu.SMEM)
    vmem = pl.BlockSpec(memory_space=pltpu.VMEM)
    anywhere = pl.BlockSpec(memory_space=pl.ANY)
    n_ch, n_au, n_vert = (lax.axis_size(axis) for axis in ("ch", "au", "vert"))
    here = screens.shape[0]
    parity = lax.rem(lax.axis_index("vert"), 2)
    chosen = lax.dynamic_slice_in_dim(screens, parity * (here // 2), here // 2, 0)
    near_half = lax.ppermute(chosen, "ch", [(i, (i + 1) % n_ch) for i in range(n_ch)])
    far_half = lax.ppermute(near_half, "vert", [(i, i ^ 1) for i in range(n_vert)])

    packed, meta = pl.pallas_call(
        pack_kernel,
        out_shape=(
            jax.ShapeDtypeStruct((SLOTS, 8, K), BF),
            jax.ShapeDtypeStruct((SLOTS, 128), F32),
        ),
        in_specs=[smem] * 5 + [vmem] * 2,
        out_specs=(vmem, vmem),
        scratch_shapes=[pltpu.VMEM((B_DEV, 128), F32), pltpu.SMEM((8,), jnp.int32)],
    )(
        heading[:, 0], offset_u, offset_v, baseline, station_pair, visibilities,
        tracks.transpose(1, 2, 0),
    )
    got_data, got_meta = pl.pallas_call(
        exchange_kernel,
        out_shape=(
            jax.ShapeDtypeStruct((SLOTS, 8, K), BF),
            jax.ShapeDtypeStruct((SLOTS, 128), F32),
        ),
        in_specs=[anywhere, anywhere],
        out_specs=(anywhere, anywhere),
        scratch_shapes=[
            pltpu.SemaphoreType.DMA((4, 2)),
            pltpu.SemaphoreType.DMA((4, 2)),
            pltpu.SemaphoreType.DMA((2,)),
        ],
        compiler_params=pltpu.CompilerParams(collective_id=0, has_side_effects=True),
    )(packed, meta)
    labels = [pltpu.SMEM((SLOTS, 128), F32)]
    listing = pltpu.SMEM((8, 2 * LATER), jnp.int32)
    images = pl.pallas_call(
        image_kernel,
        out_shape=jax.ShapeDtypeStruct((SLOTS + 2, 4 * S, 2 * S), BF),
        in_specs=[vmem, vmem],
        out_specs=vmem,
        scratch_shapes=labels
        + [
            pltpu.VMEM((SLOTS, 2 * K), F32),
            pltpu.VMEM((32, K), F32),
            listing,
            pltpu.SemaphoreType.DMA((1,)),
        ],
        compiler_params=pltpu.CompilerParams(vmem_limit_bytes=12 << 20),
        cost_estimate=pl.CostEstimate(
            flops=SLOTS * 2 * 256 * 512 * 128 * 8, bytes_accessed=8 << 20, transcendentals=0
        ),
    )(got_meta, got_data)
    right, left = jnp.asarray(right_table()), jnp.asarray(left_table())
    table_scratch = [pltpu.VMEM((2 * S, 256), F32), pltpu.VMEM((8, 2 * ROWS, 2 * S), BF)]
    canvas_shape = jax.ShapeDtypeStruct((8, TU + S + ROWS, TV + 128), F32)
    canvas, all_screens, edge_u, edge_v, corner = pl.pallas_call(
        early_kernel,
        out_shape=(
            canvas_shape,
            jax.ShapeDtypeStruct((2 * here, 2, S, 2 * S), BF),
            jax.ShapeDtypeStruct((8, S, TV), BF),
            jax.ShapeDtypeStruct((8, TU // 2, 128), BF),
            jax.ShapeDtypeStruct((8, S // 2, 128), BF),
        ),
        in_specs=[anywhere, vmem] + [anywhere] * 5,
        out_specs=(vmem,) * 5,
        scratch_shapes=labels
        + [pltpu.VMEM((2 * here, 4, S * S), BF)]
        + table_scratch
        + [pltpu.VMEM((2, 4 * S, 128), F32), listing, pltpu.SemaphoreType.DMA((6,))],
        compiler_params=pltpu.CompilerParams(vmem_limit_bytes=12 << 20),
    )(got_meta, images, screens, near_half, far_half, right, left)
    got_u = lax.ppermute(edge_u, "au", [(i, (i + 1) % n_au) for i in range(n_au)])
    got_v = lax.ppermute(edge_v, "vert", [(i, (i + 1) % n_vert) for i in range(n_vert)])
    diagonal = [
        (u * n_vert + v, (u + 1) % n_au * n_vert + (v + 1) % n_vert)
        for u in range(n_au)
        for v in range(n_vert)
    ]
    got_c = lax.ppermute(corner, ("au", "vert"), diagonal)
    canvas, tile = pl.pallas_call(
        late_kernel,
        out_shape=(canvas_shape, jax.ShapeDtypeStruct((8, TU, TV), F32)),
        in_specs=[anywhere] + [vmem] * 3 + [anywhere] * 2,
        out_specs=(vmem, anywhere),
        scratch_shapes=labels + table_scratch + [listing, pltpu.SemaphoreType.DMA((6,))],
        input_output_aliases={2: 0},
        compiler_params=pltpu.CompilerParams(vmem_limit_bytes=12 << 20),
        cost_estimate=pl.CostEstimate(
            flops=SLOTS * 2 * 256 * 512 * 128 * 8, bytes_accessed=8 << 20, transcendentals=0
        ),
    )(got_meta, images, canvas, all_screens, right, left)
    out = pl.pallas_call(
        finish_kernel,
        out_shape=jax.ShapeDtypeStruct((8, TU, TV), F32),
        in_specs=[anywhere] + [vmem] * 4,
        out_specs=anywhere,
        scratch_shapes=[
            pltpu.VMEM((8, S, TV), F32),
            pltpu.VMEM((8, TU - S, 128), F32),
            pltpu.SemaphoreType.DMA((2,)),
        ],
        input_output_aliases={0: 0},
        compiler_params=pltpu.CompilerParams(vmem_limit_bytes=8 << 20),
    )(tile, canvas, got_u, got_v, got_c)
    return out[None]


def solution(mesh):
    placed = (
        P(("au", "vert"), None, "ch"),
        P(("au", "vert"), None, None),
        P(("au", "vert")),
        P(("au", "vert")),
        P(("au", "vert"), None),
        P(("au", "vert")),
        P(),
        P("ch", None, None),
    )
    return jax.shard_map(
        body, mesh=mesh, in_specs=placed, out_specs=P("ch", None, "au", "vert"), check_vma=False
    )
```

```python
import math

import jax
import jax.numpy as jnp
import ml_dtypes
import numpy as np
from jax import lax
from jax.experimental import pallas as pl
from jax.experimental.pallas import tpu as pltpu
from jax.sharding import PartitionSpec as P

S = 64
CH_DEV = 32
TB = 8
K = TB * CH_DEV
B_DEV = 32
CAP = B_DEV // 4
SLOTS = 5 * CAP
TU = 256
TV = 256
ROWS = 72
LATER = 48
MESH = pl.DeviceIdType.MESH
BF = jnp.bfloat16
F32 = jnp.float32


def series(values, degree):
    nodes = (np.cos(np.pi * (np.arange(400) + 0.5) / 400) + 1.0) * 0.125
    fitted = np.polynomial.chebyshev.Chebyshev.fit(nodes, values(nodes), degree, domain=[0, 0.25])
    return [float(c) for c in fitted.convert(kind=np.polynomial.Polynomial).coef]


COS_COEF = series(lambda q: np.cos(2 * np.pi * np.sqrt(q)), 7)
SIN_COEF = series(lambda q: np.sin(2 * np.pi * np.sqrt(q)) / np.sqrt(q), 6)


def horner(coefs, q):
    total = jnp.full_like(q, coefs[-1])
    for c in coefs[-2::-1]:
        total = total * q + jnp.float32(c)
    return total


def dft_tables():
    centred = np.arange(S) - S // 2
    product = (centred[:, None] * centred[None, :]) % S
    angles = np.float32(2.0 * math.pi / S) * product.astype(np.float32)
    scale = np.float32(1.0 / math.sqrt(S))
    re = (np.cos(angles) * scale).astype(ml_dtypes.bfloat16).astype(np.float32)
    im = (-np.sin(angles) * scale).astype(ml_dtypes.bfloat16).astype(np.float32)
    return re, im


def right_table():
    re, im = dft_tables()
    norm = np.float32(1.0 / math.sqrt(K))
    table = np.zeros((2 * S, 256), np.float32)
    table[:S, :S] = re.T * norm
    table[S:, :S] = im.T * norm
    return table


def left_table():
    re, im = dft_tables()
    order = np.concatenate([np.arange(0, S, 2), np.arange(1, S, 2)])
    re, im = re[:, order], im[:, order]
    table = np.zeros((8, 2, ROWS, 2 * S), np.float32)
    for shift in range(8):
        table[shift, 0, shift : shift + S, :S] = re
        table[shift, 0, shift : shift + S, S:] = -im
        table[shift, 1, shift : shift + S, :S] = im
        table[shift, 1, shift : shift + S, S:] = re
    return table.reshape(8, 2 * ROWS, 2 * S).astype(ml_dtypes.bfloat16)


def pack_kernel(head, off_u, off_v, base, pairs, data, track, out_data, out_meta, rows, counts):
    for h in range(5):
        counts[h] = 0
    out_meta[...] = jnp.zeros_like(out_meta)
    lane = lax.broadcasted_iota(jnp.int32, (TB, 128), 1)
    time = lax.broadcasted_iota(jnp.int32, (TB, 128), 0)
    dims = (((0,), (0,)), ((), ()))
    rows[...] = sum(
        lax.dot_general(
            track[a],
            jnp.where(lane == time + 8 * (a + 1), 1.0, 0.0).astype(BF),
            dims,
            preferred_element_type=F32,
        )
        for a in range(2)
    )
    lane = lax.broadcasted_iota(jnp.int32, (1, 128), 1)

    def one(b, carry):
        h = head[b]
        slot = h * CAP + counts[h]
        counts[h] = counts[h] + 1
        out_data[slot] = data[b]
        label = base[b]
        row = jnp.where(lane == 0, 1, 0)
        row = jnp.where(lane == 1, off_u[b], row)
        row = jnp.where(lane == 2, off_v[b], row)
        row = jnp.where(lane == 3, pairs[0, label], row)
        row = jnp.where(lane == 4, pairs[1, label], row)
        out_meta[pl.ds(slot, 1), :] = rows[pl.ds(b, 1), :] + row.astype(F32)
        return carry

    lax.fori_loop(0, B_DEV, one, 0)


def exchange_kernel(data, meta, got_data, got_meta, send_sems, recv_sems, own_sems):
    au, vert = lax.axis_index("au"), lax.axis_index("vert")
    n_au, n_vert = lax.axis_size("au"), lax.axis_size("vert")
    near = (
        {"au": lax.rem(au + 1, n_au)},
        {"au": lax.rem(au + n_au - 1, n_au)},
        {"vert": lax.rem(vert + 1, n_vert)},
        {"vert": lax.rem(vert + n_vert - 1, n_vert)},
    )
    copies = []
    for j, (source, target) in enumerate(((data, got_data), (meta, got_meta))):
        copy = pltpu.make_async_copy(
            source.at[pl.ds(0, CAP)], target.at[pl.ds(0, CAP)], own_sems.at[j]
        )
        copy.start()
        copies.append(copy)
    barrier = pltpu.get_barrier_semaphore()
    for device in near:
        pl.semaphore_signal(barrier, inc=1, device_id=device, device_id_type=MESH)
    pl.semaphore_wait(barrier, 4)
    for i, device in enumerate(near):
        for j, (source, target) in enumerate(((data, got_data), (meta, got_meta))):
            copy = pltpu.make_async_remote_copy(
                src_ref=source.at[pl.ds((i + 1) * CAP, CAP)],
                dst_ref=target.at[pl.ds((i + 1) * CAP, CAP)],
                send_sem=send_sems.at[i, j],
                recv_sem=recv_sems.at[i, j],
                device_id=device,
                device_id_type=MESH,
            )
            copy.start()
            copies.append(copy)
    for copy in copies:
        copy.wait()


def swap_halves(x):
    return pltpu.roll(x, S, x.ndim - 1)


def enlist_blocks(labels, listing):
    def place(slot, read, counts):
        filled = read(0)
        off_u, off_v = read(1), read(2)
        past = jnp.logical_or(off_u > TU - S, off_v > TV - S)
        index = jnp.where(past, counts[0], LATER + counts[1])

        @pl.when(filled == 1)
        def _():
            listing[0, index] = slot
            listing[1, index] = off_u
            listing[2, index] = off_v
            listing[3, index] = read(3)
            listing[4, index] = read(4)

        early = jnp.where(past, filled, 0)
        return counts[0] + early, counts[1] + filled - early

    def one(slot, counts):
        return place(slot, lambda c: labels[slot, c].astype(jnp.int32), counts)

    counts = lax.fori_loop(0, SLOTS, one, (jnp.int32(0), jnp.int32(0)))
    for start, number in zip((0, LATER), counts):

        @pl.when(number % 2 == 1)
        def _():
            for column in range(5):
                listing[column, start + number] = listing[column, start + number - 1]
            listing[1, start + number] = TU + S

    return (counts[0] + 1) // 2, (counts[1] + 1) // 2


def arrange_station(raw, tall):
    value = raw.astype(F32)
    for i in range(S // 2):
        tall[8 * i : 8 * i + 4, :] = value[:, 128 * i : 128 * (i + 1)]
    lane = lax.broadcasted_iota(jnp.int32, (S // 2, 128), 1)
    feeds = []
    for f in range(2):
        re = tall[pl.ds(2 * f, S // 2, stride=8), :]
        im = tall[pl.ds(2 * f + 1, S // 2, stride=8), :]
        even = jnp.where(lane < S, re, swap_halves(im))
        odd = jnp.where(lane < S, swap_halves(re), im)
        feeds.append(jnp.concatenate([even, odd], axis=0).astype(BF))
    return feeds


def image_kernel(
    meta, data, own_screens, images, arranged, labels, spread, tall, mult, listing, sems
):
    copy = pltpu.make_async_copy(meta, labels, sems.at[0])
    copy.start()
    band = lax.axis_index("ch")
    channels = CH_DEV * lax.axis_size("ch")
    row = lax.broadcasted_iota(jnp.int32, (32, K), 0)
    channel = band * CH_DEV + lax.broadcasted_iota(jnp.int32, (32, K), 1) % CH_DEV
    ratio = 1.0 + channel.astype(F32) / jnp.float32(2 * channels)
    coarse = row - 8
    coarse_u = 16 * (coarse % 4) + coarse // 4 - S // 2
    fine_v = row - 16
    coarse_v = (row - 24) * 8 - S // 2
    step = jnp.where(
        row < 16, jnp.where(row < 8, 2 * row, coarse_u), jnp.where(row < 24, fine_v, coarse_v)
    )
    mult[...] = step.astype(F32) / S * ratio
    source = lax.broadcasted_iota(jnp.int32, (128, 2 * K), 0)
    column = lax.broadcasted_iota(jnp.int32, (128, 2 * K), 1)
    chosen = jnp.where(source == 8 + column // CH_DEV, 1.0, 0.0).astype(BF)
    lane = lax.broadcasted_iota(jnp.int32, (SLOTS, 128), 1)
    only = jnp.where(lane < 8, 0.0, meta[...]).astype(BF)
    spread[...] = jnp.dot(only, chosen, preferred_element_type=F32)
    copy.wait()
    early, late = enlist_blocks(labels, listing)

    def block(index):
        slot = listing[0, index]
        sample = data[slot].astype(F32)
        track = spread[pl.ds(slot, 1), :]
        turns = jnp.concatenate(
            [track[:, :K] * mult[:16], track[:, K:] * mult[16:]], axis=0
        )
        frac = turns - jnp.floor(turns + 0.5)
        square = frac * frac
        cos = horner(COS_COEF, square)
        sin = horner(SIN_COEF, square) * frac

        def phasors(first):
            cos_fine, sin_fine = cos[first : first + 8], sin[first : first + 8]
            all_cos, all_sin = [], []
            for a in range(8):
                at = first + 8 + a
                cos_a, sin_a = cos[at : at + 1], sin[at : at + 1]
                all_cos.append(cos_fine * cos_a - sin_fine * sin_a)
                all_sin.append(sin_fine * cos_a + cos_fine * sin_a)
            return (
                jnp.concatenate(all_cos, axis=0).astype(BF),
                jnp.concatenate(all_sin, axis=0).astype(BF),
            )

        cos_u, sin_u = phasors(0)
        cos_u, sin_u = cos_u.astype(F32), sin_u.astype(F32)
        cos_v, sin_v = phasors(16)
        table_re = jnp.concatenate([cos_v, sin_v], axis=0)
        table_im = jnp.concatenate([-sin_v, cos_v], axis=0)
        weigh_re, weigh_im = [], []
        for p in range(4):
            re, im = sample[2 * p : 2 * p + 1], sample[2 * p + 1 : 2 * p + 2]
            weigh_re.append((re * cos_u - im * sin_u).astype(BF))
            weigh_im.append((re * sin_u + im * cos_u).astype(BF))
        dims = (((1,), (1,)), ((), ()))
        image = lax.dot_general(
            jnp.concatenate(weigh_re, axis=0), table_re, dims, preferred_element_type=F32
        ) + lax.dot_general(
            jnp.concatenate(weigh_im, axis=0), table_im, dims, preferred_element_type=F32
        )
        return image.astype(BF)

    def loop(pair, carry):
        at = jnp.where(pair < early, 2 * pair, LATER + 2 * (pair - early))
        first, second = block(at), block(at + 1)
        images[2 * pair] = first
        images[2 * pair + 1] = second
        return carry

    lax.fori_loop(0, early + late, loop, 0)

    def arrange(pair, carry):
        for i in range(2):
            feeds = arrange_station(own_screens[2 * pair + i], tall.at[i])
            for f in range(2):
                arranged[2 * pair + i, f] = feeds[f]
        return carry

    lax.fori_loop(0, own_screens.shape[0] // 2, arrange, 0)


def folded(x):
    middle = x.shape[1] // 2
    lane = lax.broadcasted_iota(jnp.int32, (1, 1, 128), 2)
    return jnp.where(lane < S, x[:, :middle], swap_halves(x[:, middle:])).astype(BF)


def early_kernel(
    meta, images, arranged, got_screens, right_in, left_in,
    canvas, screens, edge_u, edge_v, corner,
    labels, raw, right, left, tall, listing, sems,
):
    here = arranged.shape[0]
    meta_copies = [pltpu.make_async_copy(meta, labels, sems.at[0])]
    fetches = [
        pltpu.make_async_copy(arranged, screens.at[:here], sems.at[2]),
        pltpu.make_async_copy(got_screens, raw, sems.at[3]),
        pltpu.make_async_copy(left_in, left, sems.at[4]),
        pltpu.make_async_copy(right_in, right, sems.at[5]),
    ]
    for copy in meta_copies + fetches:
        copy.start()
    canvas[...] = jnp.zeros_like(canvas)
    for copy in meta_copies:
        copy.wait()
    early, _ = enlist_blocks(labels, listing)
    for copy in fetches:
        copy.wait()

    def arrange(pair, carry):
        for i in range(2):
            feeds = arrange_station(raw[2 * pair + i], tall.at[i])
            for f in range(2):
                screens[here + 2 * pair + i, f] = feeds[f]
        return carry

    lax.fori_loop(0, here // 2, arrange, 0)
    grid_blocks(images, screens, canvas, right, left, listing, early, 0, 0)
    edge_u[...] = canvas[:, TU : TU + S, :TV].astype(BF)
    edge_v[...] = folded(canvas[:, :TU, TV:])
    corner[...] = folded(canvas[:, TU : TU + S, TV:])


def late_kernel(
    meta, images, canvas_in, screens, right_in, left_in,
    canvas, tile,
    labels, right, left, listing, sems,
):
    meta_copies = [pltpu.make_async_copy(meta, labels, sems.at[0])]
    fetches = [
        pltpu.make_async_copy(left_in, left, sems.at[2]),
        pltpu.make_async_copy(right_in, right, sems.at[3]),
    ]
    for copy in meta_copies + fetches:
        copy.start()
    for copy in meta_copies:
        copy.wait()
    early, late = enlist_blocks(labels, listing)
    for copy in fetches:
        copy.wait()
    grid_blocks(
        images, screens, canvas, right, left, listing, late, LATER, 2 * early
    )
    store = pltpu.make_async_copy(canvas.at[:, :TU, :TV], tile, sems.at[4])
    store.start()
    store.wait()


def grid_blocks(
    images, screens, canvas, right, left, listing, pairs, first, first_image
):
    here = screens.shape[0] // 2
    band = lax.axis_index("ch")

    def screen_place(station):
        owner = station // here
        local = station - owner * here
        return jnp.where(owner == band, local, here + local)

    def block(number):
        index = first + number
        off_u = listing[1, index]
        off_v = listing[2, index]
        one = screen_place(listing[3, index])
        two = screen_place(listing[4, index])
        two_s = [screens[two, f].astype(F32) for f in range(2)]
        fixed = []
        for f in range(2):
            one_s = screens[one, f].astype(F32)
            one_swapped = swap_halves(one_s)
            for e in range(2):
                p = 2 * f + e
                same = one_s * two_s[e]
                cross = one_swapped * two_s[e]
                gain_re = same + swap_halves(same)
                gain_im = swap_halves(cross) - cross
                part = images[first_image + number, p * S : (p + 1) * S].astype(F32)
                fixed.append((part * gain_re + swap_halves(part) * gain_im).astype(BF))
        lanes = off_v // 128
        moved = pltpu.roll(right[...], off_v - lanes * 128, 1).astype(BF)
        table_re, table_im = moved[:S], moved[S:]
        shifted = jnp.concatenate(
            [
                jnp.concatenate([table_re, -table_im], axis=0),
                jnp.concatenate([table_im, table_re], axis=0),
            ],
            axis=1,
        )
        half = jnp.dot(
            jnp.concatenate(fixed, axis=0), shifted, preferred_element_type=F32
        ).astype(BF)
        eighth = off_u // 8
        placed = left[off_u - eighth * 8]
        start_u = pl.multiple_of(eighth * 8, 8)
        start_v = pl.multiple_of(lanes * 128, 128)
        return start_u, start_v, placed, half

    def loop(pair, carry):
        ready = [block(2 * pair), block(2 * pair + 1)]
        for start_u, start_v, placed, half in ready:
            for p in range(4):
                part = half[p * S : (p + 1) * S]
                both = jnp.concatenate([part[:, :256], part[:, 256:]], axis=0)
                grid = jnp.dot(placed, both, preferred_element_type=F32)
                for r in range(2):
                    where = (2 * p + r, pl.ds(start_u, ROWS), pl.ds(start_v, 256))
                    canvas[where] += grid[r * ROWS : (r + 1) * ROWS]
        return carry

    lax.fori_loop(0, pairs, loop, 0)


def finish_kernel(tile, canvas, got_u, got_v, got_c, out, top, side, sems):
    lane = lax.broadcasted_iota(jnp.int32, (1, 1, 128), 2)

    def unfolded(x):
        x = x.astype(F32)
        low = jnp.where(lane < S, x, 0.0)
        high = jnp.where(lane < S, swap_halves(x), 0.0)
        return low, high

    low, high = unfolded(got_v[...])
    first, second = unfolded(got_c[...])
    top[...] = canvas[:, :S, :TV] + got_u[...].astype(F32)
    top[:, :, :128] += low[:, :S] + jnp.concatenate([first, second], axis=1)
    store_top = pltpu.make_async_copy(top, out.at[:, :S, :], sems.at[0])
    store_top.start()
    side[:, : TU // 2 - S] = canvas[:, S : TU // 2, :128] + low[:, S:]
    side[:, TU // 2 - S :] = canvas[:, TU // 2 : TU, :128] + high
    store_side = pltpu.make_async_copy(side, out.at[:, S:, :128], sems.at[1])
    store_side.start()
    store_top.wait()
    store_side.wait()


def body(visibilities, tracks, offset_u, offset_v, heading, baseline, station_pair, screens):
    smem = pl.BlockSpec(memory_space=pltpu.SMEM)
    vmem = pl.BlockSpec(memory_space=pltpu.VMEM)
    anywhere = pl.BlockSpec(memory_space=pl.ANY)
    n_ch, n_au, n_vert = (lax.axis_size(axis) for axis in ("ch", "au", "vert"))
    here = screens.shape[0]
    got_screens = lax.ppermute(screens, "ch", [(i, (i + 1) % n_ch) for i in range(n_ch)])

    packed, meta = pl.pallas_call(
        pack_kernel,
        out_shape=(
            jax.ShapeDtypeStruct((SLOTS, 8, K), BF),
            jax.ShapeDtypeStruct((SLOTS, 128), F32),
        ),
        in_specs=[smem] * 5 + [vmem] * 2,
        out_specs=(vmem, vmem),
        scratch_shapes=[pltpu.VMEM((B_DEV, 128), F32), pltpu.SMEM((8,), jnp.int32)],
    )(
        heading[:, 0], offset_u, offset_v, baseline, station_pair, visibilities,
        tracks.transpose(1, 2, 0),
    )
    got_data, got_meta = pl.pallas_call(
        exchange_kernel,
        out_shape=(
            jax.ShapeDtypeStruct((SLOTS, 8, K), BF),
            jax.ShapeDtypeStruct((SLOTS, 128), F32),
        ),
        in_specs=[anywhere, anywhere],
        out_specs=(anywhere, anywhere),
        scratch_shapes=[
            pltpu.SemaphoreType.DMA((4, 2)),
            pltpu.SemaphoreType.DMA((4, 2)),
            pltpu.SemaphoreType.DMA((2,)),
        ],
        compiler_params=pltpu.CompilerParams(collective_id=0, has_side_effects=True),
    )(packed, meta)
    labels = [pltpu.SMEM((SLOTS, 128), F32)]
    listing = pltpu.SMEM((8, 2 * LATER), jnp.int32)
    images, arranged = pl.pallas_call(
        image_kernel,
        out_shape=(
            jax.ShapeDtypeStruct((SLOTS + 2, 4 * S, 2 * S), BF),
            jax.ShapeDtypeStruct((here, 2, S, 2 * S), BF),
        ),
        in_specs=[vmem] * 3,
        out_specs=(vmem, vmem),
        scratch_shapes=labels
        + [
            pltpu.VMEM((SLOTS, 2 * K), F32),
            pltpu.VMEM((2, 4 * S, 128), F32),
            pltpu.VMEM((32, K), F32),
            listing,
            pltpu.SemaphoreType.DMA((1,)),
        ],
        compiler_params=pltpu.CompilerParams(vmem_limit_bytes=12 << 20),
        cost_estimate=pl.CostEstimate(
            flops=SLOTS * 2 * 256 * 512 * 128 * 8, bytes_accessed=8 << 20, transcendentals=0
        ),
    )(got_meta, got_data, screens)
    right, left = jnp.asarray(right_table()), jnp.asarray(left_table())
    table_scratch = [pltpu.VMEM((2 * S, 256), F32), pltpu.VMEM((8, 2 * ROWS, 2 * S), BF)]
    canvas_shape = jax.ShapeDtypeStruct((8, TU + S + ROWS, TV + 128), F32)
    canvas, all_screens, edge_u, edge_v, corner = pl.pallas_call(
        early_kernel,
        out_shape=(
            canvas_shape,
            jax.ShapeDtypeStruct((2 * here, 2, S, 2 * S), BF),
            jax.ShapeDtypeStruct((8, S, TV), BF),
            jax.ShapeDtypeStruct((8, TU // 2, 128), BF),
            jax.ShapeDtypeStruct((8, S // 2, 128), BF),
        ),
        in_specs=[anywhere, vmem] + [anywhere] * 4,
        out_specs=(vmem,) * 5,
        scratch_shapes=labels
        + [pltpu.VMEM((here, 4, S * S), BF)]
        + table_scratch
        + [pltpu.VMEM((2, 4 * S, 128), F32), listing, pltpu.SemaphoreType.DMA((6,))],
        compiler_params=pltpu.CompilerParams(vmem_limit_bytes=12 << 20),
    )(got_meta, images, arranged, got_screens, right, left)
    got_u = lax.ppermute(edge_u, "au", [(i, (i + 1) % n_au) for i in range(n_au)])
    got_v = lax.ppermute(edge_v, "vert", [(i, (i + 1) % n_vert) for i in range(n_vert)])
    diagonal = [
        (u * n_vert + v, (u + 1) % n_au * n_vert + (v + 1) % n_vert)
        for u in range(n_au)
        for v in range(n_vert)
    ]
    got_c = lax.ppermute(corner, ("au", "vert"), diagonal)
    canvas, tile = pl.pallas_call(
        late_kernel,
        out_shape=(canvas_shape, jax.ShapeDtypeStruct((8, TU, TV), F32)),
        in_specs=[anywhere] + [vmem] * 3 + [anywhere] * 2,
        out_specs=(vmem, anywhere),
        scratch_shapes=labels + table_scratch + [listing, pltpu.SemaphoreType.DMA((6,))],
        input_output_aliases={2: 0},
        compiler_params=pltpu.CompilerParams(vmem_limit_bytes=12 << 20),
        cost_estimate=pl.CostEstimate(
            flops=SLOTS * 2 * 256 * 512 * 128 * 8, bytes_accessed=8 << 20, transcendentals=0
        ),
    )(got_meta, images, canvas, all_screens, right, left)
    out = pl.pallas_call(
        finish_kernel,
        out_shape=jax.ShapeDtypeStruct((8, TU, TV), F32),
        in_specs=[anywhere] + [vmem] * 4,
        out_specs=anywhere,
        scratch_shapes=[
            pltpu.VMEM((8, S, TV), F32),
            pltpu.VMEM((8, TU - S, 128), F32),
            pltpu.SemaphoreType.DMA((2,)),
        ],
        input_output_aliases={0: 0},
        compiler_params=pltpu.CompilerParams(vmem_limit_bytes=8 << 20),
    )(tile, canvas, got_u, got_v, got_c)
    return out[None]


def solution(mesh):
    placed = (
        P(("au", "vert"), None, "ch"),
        P(("au", "vert"), None, None),
        P(("au", "vert")),
        P(("au", "vert")),
        P(("au", "vert"), None),
        P(("au", "vert")),
        P(),
        P("ch", None, None),
    )
    return jax.shard_map(
        body, mesh=mesh, in_specs=placed, out_specs=P("ch", None, "au", "vert"), check_vma=False
    )
```
